32 devices in a mesh: req: 8 (over z, y), tp: 4 (over x, core).
Axes of the slice: x: 2, y: 2, z: 4, core: 2. Of those that a mesh axis runs over, the one named last changes fastest.
Arguments:
- residual: bfloat16 [256, 2048], P('req'), may hold values from -6 to 6
- cache_lengths: int32 [256], P('req'), may hold values from 4 to 4096, as said below
- input_gain: float32 [2048], replicated, may hold values from 0.1 to 1.9
- inner_weight: bfloat16 [2048, 2, 1536], P(None, None, 'tp'), may hold values from -0.125 to 0.125
- step_weight: bfloat16 [2048, 24], P(None, 'tp'), may hold values from -0.125 to 0.125
- step_bias: float32 [24], P('tp'), may hold values from -4 to -1
- decay_log: float32 [24], P('tp'), may hold values from 0 to 2.77
- skip_gain: float32 [24], P('tp'), may hold values from 0.5 to 2
- conv_weight: bfloat16 [4, 1536], P(None, 'tp'), may hold values from -3 to 3
- conv_state: bfloat16 [256, 3, 1536], P('req', None, 'tp'), may hold values from -6 to 6
- coupling_weight: bfloat16 [2048, 512], P(None, 'tp'), may hold values from -0.125 to 0.125
- coupling_conv: bfloat16 [4, 512], P(None, 'tp'), may hold values from -3 to 3
- coupling_state: bfloat16 [256, 3, 512], P('req', None, 'tp'), may hold values from -6 to 6
- scan_state: bfloat16 [256, 24, 64, 256], P('req', 'tp'), may hold values from -30 to 30
- mixer_gain: float32 [1536], P('tp'), may hold values from 0.1 to 1.9
- attention_weight: bfloat16 [2048, 1536], P(None, 'tp'), may hold values from -0.125 to 0.125
- sink_cache: bfloat16 [256, 4, 512], P('req'), may hold values from -2000 to 2000
- window_cache: bfloat16 [256, 1024, 512], P('req', 'tp'), may hold values from -9 to 9
- mamba_out: bfloat16 [1536, 2048], P('tp'), may hold values from -0.15625 to 0.15625
- attention_out: bfloat16 [1024, 2048], P('tp'), may hold values from -0.5 to 0.5
- final_gain: float32 [2048], replicated, may hold values from 0.1 to 1.9
- output_head: bfloat16 [2048, 65536], P(None, ('req', 'tp')), may hold values from -0.375 to 0.375
Outputs:
- new_residual: bfloat16 [256, 2048], P('req', 'tp')
- logits: float32 [256, 65536], P(('req', 'tp'))
- new_scan_state: bfloat16 [256, 24, 64, 256], P('req', 'tp')
- new_conv_state: bfloat16 [256, 3, 1536], P('req', None, 'tp')
- new_coupling_state: bfloat16 [256, 3, 512], P('req', None, 'tp')
- new_key_value: bfloat16 [256, 512], P('req')
The draws below stay inside these ranges and needn't reach their ends.
Inputs may be any that keep to these rules, and one draw needn't show every extreme that they name: `cache_lengths`: A request's cache holds positions 0 to its length - 1; the new token stands at the position equal to the length. Some request has length exactly 4096.
All inputs are finite; a program needn't handle non-finite values.
Results may differ from the reference program's by a relative error of at most 0.02.
Values may be sent and summed in bfloat16 or wider, within the bound.
A program may use at most 128 MiB of HBM per device.

```python
import jax
import jax.numpy as jnp
from jax import lax

D = 2048
MH = 24
MP = 64
NS = 256
CONV = 4
QH = 8
KVH = 2
HD = 128
VOCAB = 65536
WIN = 1024
SINK = 4
MAXLEN = 4096
REQS = 256
DSSM = 1536
QKV = 1536


def draw_cache_lengths(key, part):
    first_draw = jax.random.randint(jax.random.fold_in(key, 11), (REQS,), 0, MAXLEN)
    second_draw = jax.random.randint(jax.random.fold_in(key, 12), (REQS,), 0, MAXLEN)
    drawn = jnp.minimum(SINK + first_draw * second_draw // MAXLEN, MAXLEN)
    chosen = jax.random.randint(jax.random.fold_in(key, 13), (), 0, REQS)
    return jnp.where(jnp.arange(REQS) == chosen, MAXLEN, drawn).astype(jnp.int32)


def draw_scan_state(key, part):
    sampled = jax.random.normal(jax.random.fold_in(key, 21), (REQS, MH, MP, NS), jnp.float32)
    head_level = jnp.arange(MH, dtype=jnp.float32) / max(MH - 1, 1)
    rising = 0.05 * jnp.exp(2.302585 * head_level)
    row_level = jnp.exp(jax.random.uniform(jax.random.fold_in(key, 22), (REQS,), jnp.float32, 0.0, 2.3))
    scaled = sampled * (row_level[:, None] * rising[None, :])[:, :, None, None]
    return jnp.clip(scaled, -29.5, 29.5).astype(jnp.bfloat16)


def draw_sink_cache(key, part):
    half_width = KVH * HD
    sampled = 1.5 * jax.random.normal(jax.random.fold_in(key, 31), (REQS, SINK, 2 * half_width), jnp.float32)
    return jnp.clip(sampled, -1990.0, 1990.0).astype(jnp.bfloat16)


def shard_levels(key, dims, split, low, high):
    loudness = 1.0
    for axis_at, shards_of in split:
        draws = jax.random.uniform(jax.random.fold_in(jax.random.fold_in(key, 6), axis_at), (shards_of,), jnp.float32, low / len(split), high / len(split))
        loudness = loudness * jnp.repeat(jnp.exp(draws), dims[axis_at] // shards_of).reshape((-1,) + (1,) * (len(dims) - 1 - axis_at))
    return loudness


def gaussian(stream_key, shape, scale, most, pieces=(), kind=jnp.bfloat16):
    level = shard_levels(stream_key, shape, pieces, -0.22, 0.18) if pieces else 1.0
    values = jax.random.normal(stream_key, shape, jnp.float32) * scale * level
    return jnp.minimum(jnp.maximum(values, -most), most).astype(kind)


def setup_inputs(seed: int = 0) -> dict:
    streams_of = jax.random.split(jax.random.key(seed), 23)
    return {
        "residual": gaussian(streams_of[0], (REQS, D), 1.0, 6.0, ((0, 8),)),
        "cache_lengths": draw_cache_lengths(jax.random.fold_in(streams_of[22], 71), 0),
        "input_gain": jnp.clip(1.0 + 0.18 * jax.random.normal(streams_of[2], (D,), jnp.float32), 0.1, 1.9),
        "inner_weight": gaussian(streams_of[3], (D, 2, DSSM), D ** -0.5, 0.125, ((2, 4),)),
        "step_weight": gaussian(streams_of[4], (D, MH), D ** -0.5, 0.125, ((1, 4),)),
        "step_bias": jnp.clip(-4.0 + 3.0 * jax.random.uniform(streams_of[5], (MH,), jnp.float32) ** shard_levels(streams_of[5], (MH,), ((0, 4),), -0.2, 0.2), -4.0, -1.0),
        "decay_log": jnp.clip(2.77 * jax.random.uniform(streams_of[6], (MH,), jnp.float32) ** shard_levels(streams_of[6], (MH,), ((0, 4),), -0.2, 0.2), 0.0, 2.77),
        "skip_gain": jnp.clip(0.5 + 1.5 * jax.random.uniform(streams_of[7], (MH,), jnp.float32) ** shard_levels(streams_of[7], (MH,), ((0, 4),), -0.2, 0.2), 0.5, 2.0),
        "conv_weight": gaussian(streams_of[8], (CONV, DSSM), CONV ** -0.5, 3.0, ((1, 4),)),
        "conv_state": gaussian(streams_of[9], (REQS, CONV - 1, DSSM), 1.0, 6.0, ((0, 8), (2, 4))),
        "coupling_weight": gaussian(streams_of[10], (D, 2 * NS), D ** -0.5, 0.125, ((1, 4),)),
        "coupling_conv": gaussian(streams_of[11], (CONV, 2 * NS), CONV ** -0.5, 3.0, ((1, 4),)),
        "coupling_state": gaussian(streams_of[12], (REQS, CONV - 1, 2 * NS), 1.0, 6.0, ((0, 8), (2, 4))),
        "scan_state": draw_scan_state(jax.random.fold_in(streams_of[22], 71), 0),
        "mixer_gain": jnp.clip(1.0 + 0.18 * jax.random.normal(streams_of[14], (DSSM,), jnp.float32), 0.1, 1.9),
        "attention_weight": gaussian(streams_of[15], (D, QKV), D ** -0.5, 0.125, ((1, 4),)),
        "sink_cache": draw_sink_cache(jax.random.fold_in(streams_of[22], 71), 0),
        "window_cache": gaussian(streams_of[17], (REQS, WIN, 2 * KVH * HD), 1.5, 9.0, ((0, 8), (1, 4))),
        "mamba_out": gaussian(streams_of[18], (DSSM, D), DSSM ** -0.5, 0.15625, ((0, 4),)),
        "attention_out": gaussian(streams_of[19], (QH * HD, D), HD ** -0.5, 0.5, ((0, 4),)),
        "final_gain": jnp.clip(1.0 + 0.18 * jax.random.normal(streams_of[20], (D,), jnp.float32), 0.1, 1.9),
        "output_head": gaussian(streams_of[21], (D, VOCAB), (D // 9) ** -0.5, 0.375, ((1, 32),)),
    }


EPSILON = 1e-05

def rounded(values):
    return lax.optimization_barrier(values.astype(jnp.bfloat16))

def rms_rows(values, gain):
    widened = values.astype(jnp.float32)
    mean_sq = lax.optimization_barrier(jnp.mean(widened * widened, axis=-1, keepdims=True))
    return (widened * lax.rsqrt(mean_sq + EPSILON) * gain).astype(jnp.bfloat16)

def conv_apply(old_state, fresh_row, taps):
    window = jnp.concatenate([old_state, fresh_row[:, None, :]], axis=1)
    mixed_rows = jnp.einsum('rkc,kc->rc', window.astype(jnp.float32), taps.astype(jnp.float32), precision=lax.Precision.HIGHEST)
    return (jax.nn.silu(mixed_rows), window[:, 1:, :])

def scan_request(operands):
    old_state, x_heads, step_size, decay_rate, input_vec, output_vec = operands
    updated = decay_rate[:, None, None] * old_state.astype(jnp.float32) + (step_size[:, None] * x_heads)[:, :, None] * input_vec[None, None, :]
    readout = jnp.einsum('hpn,n->hp', updated, output_vec, precision=lax.Precision.HIGHEST)
    return (updated.astype(jnp.bfloat16), readout)

def attend_request(operands):
    qkv_row, sinks, window_rows, length = operands
    half_width = KVH * HD
    queries = qkv_row[:QH * HD].reshape(KVH, QH // KVH, HD).astype(jnp.float32)
    fresh_row = qkv_row[QH * HD:].reshape(1, 2 * half_width)
    stacked = jnp.concatenate([sinks, window_rows, fresh_row], axis=0).astype(jnp.float32)
    key_rows = stacked[:, :half_width].reshape(-1, KVH, HD)
    value_rows = stacked[:, half_width:].reshape(-1, KVH, HD)
    slot_index = jnp.arange(WIN, dtype=jnp.int32)
    back_steps = (length - 1 - slot_index) % WIN
    live_slots = (length - 1 - back_steps >= SINK) & (back_steps != WIN - 1)
    valid_mask = jnp.concatenate([jnp.ones((SINK,), dtype=jnp.bool_), live_slots, jnp.ones((1,), dtype=jnp.bool_)])
    scores = jnp.einsum('kgd,skd->kgs', queries, key_rows, precision=lax.Precision.HIGHEST) * HD ** (-0.5)
    masked = jnp.where(valid_mask, scores, -jnp.inf)
    row_peak = lax.optimization_barrier(jnp.max(masked, axis=-1, keepdims=True))
    weights = jnp.where(valid_mask, jnp.exp(masked - row_peak), 0.0)
    totals = lax.optimization_barrier(jnp.sum(weights, axis=-1))
    summed = jnp.einsum('kgs,skd->kgd', rounded(weights).astype(jnp.float32), value_rows, precision=lax.Precision.HIGHEST)
    return (summed / totals[..., None]).reshape(QH * HD).astype(jnp.bfloat16)

def reference(residual, cache_lengths, input_gain, inner_weight, step_weight, step_bias, decay_log, skip_gain, conv_weight, conv_state, coupling_weight, coupling_conv, coupling_state, scan_state, mixer_gain, attention_weight, sink_cache, window_cache, mamba_out, attention_out, final_gain, output_head):
    units = MH * MP
    normed = rms_rows(residual, input_gain)
    projected = rounded(jnp.dot(normed, inner_weight.reshape(D, 2 * units), preferred_element_type=jnp.float32))
    gate_rows = projected[:, :units]
    x_rows, new_conv_state = conv_apply(conv_state, projected[:, units:], conv_weight)
    step_rows = rounded(jnp.dot(normed, step_weight, preferred_element_type=jnp.float32))
    step_size = jax.nn.softplus(step_rows.astype(jnp.float32) + step_bias)
    decay_rate = jnp.exp(-step_size * jnp.exp(decay_log))
    coupling_pre = rounded(jnp.dot(normed, coupling_weight, preferred_element_type=jnp.float32))
    coupling_rows, new_coupling_state = conv_apply(coupling_state, coupling_pre, coupling_conv)
    coupling_rows = rounded(coupling_rows).astype(jnp.float32)
    x_heads = x_rows.reshape(REQS, MH, MP)
    new_scan_state, readout = lax.map(scan_request, (scan_state, x_heads, step_size, decay_rate, coupling_rows[:, :NS], coupling_rows[:, NS:]))
    readout = readout + skip_gain[None, :, None] * x_heads
    gated_rows = readout.reshape(REQS, units) * jax.nn.silu(gate_rows.astype(jnp.float32))
    mean_sq = lax.optimization_barrier(jnp.mean(gated_rows * gated_rows, axis=1, keepdims=True))
    mamba_rows = (gated_rows * lax.rsqrt(mean_sq + EPSILON) * mixer_gain).astype(jnp.bfloat16)
    qkv_rows = rounded(jnp.dot(normed, attention_weight, preferred_element_type=jnp.float32))
    new_key_value = qkv_rows[:, QH * HD:]
    attended = lax.map(attend_request, (qkv_rows, sink_cache, window_cache, cache_lengths))
    mixed_rows = jnp.dot(mamba_rows, mamba_out, preferred_element_type=jnp.float32) + jnp.dot(attended, attention_out, preferred_element_type=jnp.float32)
    new_residual = (residual.astype(jnp.float32) + mixed_rows).astype(jnp.bfloat16)
    final_rows = rms_rows(new_residual, final_gain)
    logits = jnp.dot(final_rows, output_head, preferred_element_type=jnp.float32)
    return (new_residual, logits, new_scan_state, new_conv_state, new_coupling_state, new_key_value)
```

```python
import functools

import jax
import jax.numpy as jnp
from jax import lax
from jax.experimental import pallas as pl
from jax.experimental.pallas import tpu as pltpu
from jax.sharding import PartitionSpec as P

MH = 24
MP = 64
NS = 256
QH = 8
KVH = 2
HD = 128
WIN = 1024
SINK = 4
BR = 8
EXTRA = 16

EPSILON = 1e-05
NEG_BIG = -1e30
MESH = pl.DeviceIdType.MESH
NT = (((1,), (1,)), ((), ()))


def norm_rows(values, gain):
    widened = values.astype(jnp.float32)
    mean_sq = jnp.mean(widened * widened, axis=-1, keepdims=True)
    return (widened * lax.rsqrt(mean_sq + EPSILON) * gain).astype(jnp.bfloat16)


def conv_apply(old_state, fresh_row, taps):
    window = jnp.concatenate([old_state, fresh_row[:, None, :]], axis=1)
    mixed_rows = jnp.einsum("rkc,kc->rc", window, taps, preferred_element_type=jnp.float32)
    return (jax.nn.silu(mixed_rows), window[:, 1:, :])


def mixer_kernel(
    qkv_ref, extra_ref, mask_ref, window_ref, state_ref, coup_ref, x_ref, step_ref, decay_ref,
    gate_ref, skip_ref, new_state_ref, summed_ref, stats_ref, gated_ref, heads_scr,
):
    half = KVH * HD
    group = QH // KVH
    for h in range(QH):
        heads_scr[pl.ds(h, BR, stride=QH), :] = qkv_ref[:, h * HD : (h + 1) * HD].astype(jnp.float32)
    head_row = lax.broadcasted_iota(jnp.int32, (QH, HD), 0)
    lane = lax.broadcasted_iota(jnp.int32, (QH, HD), 1)
    first_half = head_row < group
    x = x_ref[...]
    step_x = step_ref[...] * x
    decay = decay_ref[...]
    step_x_t = step_x.T
    decay_t = decay.T
    coup = coup_ref[...]
    out_rows = coup[:, NS:]
    in_f32 = coup[:, :NS].astype(jnp.float32)
    both = jnp.sum(in_f32 * out_rows.astype(jnp.float32), axis=1, keepdims=True)
    read_rows = []
    for j in range(BR):
        q = heads_scr[j * QH : (j + 1) * QH, :]
        wide = jnp.concatenate(
            [jnp.where(first_half, q, 0.0), jnp.where(first_half, 0.0, q)], axis=1
        ).astype(jnp.bfloat16)
        s1 = lax.dot_general(
            wide, window_ref[j, :, :half], NT, preferred_element_type=jnp.float32
        ) * HD ** (-0.5)
        s2 = lax.dot_general(
            wide, extra_ref[j, :, :half], NT, preferred_element_type=jnp.float32
        ) * HD ** (-0.5)
        slots = window_ref.shape[1]
        live1 = jnp.broadcast_to(mask_ref[j : j + 1, :slots], s1.shape) > 0.5
        live2 = jnp.broadcast_to(mask_ref[j : j + 1, slots : slots + EXTRA], s2.shape) > 0.5
        s1 = jnp.where(live1, s1, NEG_BIG)
        s2 = jnp.where(live2, s2, NEG_BIG)
        peak = jnp.maximum(
            jnp.max(s1, axis=1, keepdims=True), jnp.max(s2, axis=1, keepdims=True)
        )
        w1 = jnp.where(live1, jnp.exp(s1 - peak), 0.0)
        w2 = jnp.where(live2, jnp.exp(s2 - peak), 0.0)
        total = jnp.sum(w1, axis=1, keepdims=True) + jnp.sum(w2, axis=1, keepdims=True)
        acc = jnp.dot(
            w1.astype(jnp.bfloat16), window_ref[j, :, half:], preferred_element_type=jnp.float32
        ) + jnp.dot(
            w2.astype(jnp.bfloat16), extra_ref[j, :, half:], preferred_element_type=jnp.float32
        )
        heads_scr[j * QH : (j + 1) * QH, :] = jnp.where(first_half, acc[:, :HD], acc[:, HD:])
        stats_ref[j : j + 1, :] = jnp.sum(
            jnp.where(lane == head_row, peak, 0.0)
            + jnp.where(lane == head_row + QH, total, 0.0),
            axis=0,
            keepdims=True,
        )
        state = state_ref[j]
        read_rows.append(
            lax.dot_general(out_rows, state, NT, preferred_element_type=jnp.float32)[j : j + 1, :]
        )
        new_state_ref[j] = (
            decay_t[:, j : j + 1] * state.astype(jnp.float32)
            + step_x_t[:, j : j + 1] * in_f32[j : j + 1, :]
        ).astype(jnp.bfloat16)
    per_chunk = summed_ref.shape[2] // HD
    for h in range(QH):
        summed_ref[h // per_chunk, :, (h % per_chunk) * HD : (h % per_chunk + 1) * HD] = heads_scr[
            pl.ds(h, BR, stride=QH), :
        ].astype(jnp.bfloat16)
    readout = decay * jnp.concatenate(read_rows, axis=0) + step_x * both + skip_ref[...] * x
    gate = gate_ref[...].astype(jnp.float32)
    gated = readout * (gate / (1.0 + jnp.exp(-gate)))
    gated_ref[...] = gated
    square = jnp.sum(gated * gated, axis=1, keepdims=True)
    stats_ref[...] = jnp.where(
        lax.broadcasted_iota(jnp.int32, stats_ref.shape, 1) == 2 * QH, square, stats_ref[...]
    )


def mixer(qkv, extra, mask, window, state, coup, x, step, decay, gate, skip, tp_size):
    rows, units = x.shape
    slots = window.shape[1]
    row = lambda width: pl.BlockSpec((BR, width), lambda i: (i, 0))
    cube = lambda a: pl.BlockSpec((BR,) + a.shape[1:], lambda i: (i, 0, 0))
    chunk = QH * HD // tp_size
    return pl.pallas_call(
        mixer_kernel,
        grid=(rows // BR,),
        in_specs=[
            row(qkv.shape[1]), cube(extra), row(mask.shape[1]), cube(window), cube(state),
            row(coup.shape[1]), row(units), row(units), row(units), row(units),
            pl.BlockSpec((1, units), lambda i: (0, 0)),
        ],
        out_specs=[
            cube(state), pl.BlockSpec((tp_size, BR, chunk), lambda i: (0, i, 0)), row(128), row(units),
        ],
        out_shape=[
            jax.ShapeDtypeStruct(state.shape, jnp.bfloat16),
            jax.ShapeDtypeStruct((tp_size, rows, chunk), jnp.bfloat16),
            jax.ShapeDtypeStruct((rows, 128), jnp.float32),
            jax.ShapeDtypeStruct((rows, units), jnp.float32),
        ],
        scratch_shapes=[pltpu.VMEM((BR * QH, HD), jnp.float32)],
        compiler_params=pltpu.CompilerParams(vmem_limit_bytes=40 << 20),
    )(qkv, extra, mask, window, state, coup, x, step, decay, gate, skip)


def joint_kernel(
    tp_size, req_size, summed_ref, stats_ref, gated_ref, mixer_gain_ref, mamba_out_ref,
    attention_out_ref, residual_ref, final_gain_ref, new_residual_ref, final_ref,
    sum_buf, stat_buf, part_out, part_buf, gather, sum_s, sum_r, stat_s, stat_r, part_s, part_r,
    gat_s, gat_r,
):
    r = lax.axis_index("req")
    t = lax.axis_index("tp")
    rows = gated_ref.shape[0]
    width = new_residual_ref.shape[1]
    peers = [lax.rem(t + k, tp_size) for k in range(tp_size)]
    reqs = [lax.rem(r + k, req_size) for k in range(req_size)]
    barrier = pltpu.get_barrier_semaphore()
    for k in range(1, tp_size):
        pl.semaphore_signal(barrier, inc=1, device_id=(r, peers[k]), device_id_type=MESH)
    for k in range(1, req_size):
        pl.semaphore_signal(barrier, inc=1, device_id=(reqs[k], t), device_id_type=MESH)
    pl.semaphore_wait(barrier, tp_size - 1 + req_size - 1)

    def send(src, dst, ssem, rsem, where):
        copy = pltpu.make_async_remote_copy(
            src_ref=src, dst_ref=dst, send_sem=ssem, recv_sem=rsem,
            device_id=where, device_id_type=MESH,
        )
        copy.start()
        return copy

    first = []
    for k in range(1, tp_size):
        where = (r, peers[k])
        first.append(send(stats_ref, stat_buf.at[k], stat_s.at[k], stat_r.at[k], where))
        first.append(send(summed_ref.at[peers[k]], sum_buf.at[k], sum_s.at[k], sum_r.at[k], where))
    for copy in first:
        copy.wait()
    stats = [stats_ref[...]] + [stat_buf[k] for k in range(1, tp_size)]
    sums = [summed_ref[t].astype(jnp.float32)] + [
        sum_buf[k].astype(jnp.float32) for k in range(1, tp_size)
    ]
    lane = lax.broadcasted_iota(jnp.int32, (rows, 128), 1)
    local_heads = QH // tp_size
    pieces = []
    for hl in range(local_heads):
        h = t * local_heads + hl
        peaks = [jnp.sum(jnp.where(lane == h, s, 0.0), axis=1, keepdims=True) for s in stats]
        totals = [jnp.sum(jnp.where(lane == h + QH, s, 0.0), axis=1, keepdims=True) for s in stats]
        top = functools.reduce(jnp.maximum, peaks)
        scales = [jnp.exp(p - top) for p in peaks]
        below = functools.reduce(jnp.add, [a * b for a, b in zip(scales, totals)])
        above = functools.reduce(
            jnp.add, [a * b[:, hl * HD : (hl + 1) * HD] for a, b in zip(scales, sums)]
        )
        pieces.append((above / below).astype(jnp.bfloat16))
    attended = jnp.concatenate(pieces, axis=1)
    square = functools.reduce(jnp.add, [s[:, 2 * QH : 2 * QH + 1] for s in stats])
    mamba = (
        gated_ref[...] * lax.rsqrt(square / (MH * MP) + EPSILON) * mixer_gain_ref[...]
    ).astype(jnp.bfloat16)

    def partial(p):
        cols = pl.ds(pl.multiple_of(p * width, 128), width)
        return jnp.dot(mamba, mamba_out_ref[:, cols], preferred_element_type=jnp.float32) + jnp.dot(
            attended, attention_out_ref[:, cols], preferred_element_type=jnp.float32
        )

    second = []
    for k in range(1, tp_size):
        part_out[k] = partial(peers[k]).astype(jnp.bfloat16)
        second.append(
            send(part_out.at[k], part_buf.at[k], part_s.at[k], part_r.at[k], (r, peers[k]))
        )
    mixed = partial(t)
    for k in range(1, tp_size):
        second[k - 1].wait()
        mixed = mixed + part_buf[k].astype(jnp.float32)
    own = pl.ds(pl.multiple_of(t * width, 128), width)
    fresh = (residual_ref[:, own].astype(jnp.float32) + mixed).astype(jnp.bfloat16)
    new_residual_ref[...] = fresh
    gather[0, 0] = fresh

    beside = t + 1 - 2 * lax.rem(t, 2)
    across = lax.rem(t + 2, tp_size)
    owner = [t, beside, across, lax.rem(beside + 2, tp_size)]
    along = [None]
    for k in range(1, req_size):
        along.append(
            send(gather.at[0, 0], gather.at[k, 0], gat_s.at[k, 0], gat_r.at[k, 0], (reqs[k], t))
        )
    over, near, far = [], [], []
    for k in range(req_size):
        if k:
            along[k].wait_recv()
        over.append(
            send(gather.at[k, 0], gather.at[k, 2], gat_s.at[k, 2], gat_r.at[k, 2], (r, across))
        )
        near.append(
            send(gather.at[k, 0], gather.at[k, 1], gat_s.at[k, 1], gat_r.at[k, 1], (r, beside))
        )
    for k in range(req_size):
        over[k].wait_recv()
        far.append(
            send(gather.at[k, 2], gather.at[k, 3], gat_s.at[k, 3], gat_r.at[k, 3], (r, beside))
        )
    for k in range(req_size):
        near[k].wait_recv()
        far[k].wait_recv()
        values = [gather[k, i].astype(jnp.float32) for i in range(4)]
        mean = functools.reduce(
            jnp.add, [jnp.sum(v * v, axis=1, keepdims=True) for v in values]
        ) / (width * tp_size)
        scale = lax.rsqrt(mean + EPSILON)
        source = lax.rem(r + req_size - k, req_size)
        at = pl.ds(pl.multiple_of(source * rows, rows), rows)
        for i in range(4):
            cols = pl.ds(pl.multiple_of(owner[i] * width, 128), width)
            final_ref[at, cols] = (values[i] * scale * final_gain_ref[:, cols]).astype(jnp.bfloat16)
    for k in range(req_size):
        if k:
            along[k].wait_send()
        over[k].wait_send()
        near[k].wait_send()
        far[k].wait_send()


def joint(summed, stats, gated, mixer_gain, mamba_out, attention_out, residual, final_gain):
    tp_size = lax.axis_size("tp")
    req_size = lax.axis_size("req")
    rows, model = residual.shape
    width = model // tp_size
    chunk = summed.shape[2]
    dma = lambda *shape: pltpu.SemaphoreType.DMA(shape)
    vmem = pl.BlockSpec(memory_space=pltpu.VMEM)
    return pl.pallas_call(
        functools.partial(joint_kernel, tp_size, req_size),
        in_specs=[vmem] * 8,
        out_specs=[vmem] * 2,
        out_shape=[
            jax.ShapeDtypeStruct((rows, width), jnp.bfloat16),
            jax.ShapeDtypeStruct((rows * req_size, model), jnp.bfloat16),
        ],
        scratch_shapes=[
            pltpu.VMEM((tp_size, rows, chunk), jnp.bfloat16),
            pltpu.VMEM((tp_size, rows, 128), jnp.float32),
            pltpu.VMEM((tp_size, rows, width), jnp.bfloat16),
            pltpu.VMEM((tp_size, rows, width), jnp.bfloat16),
            pltpu.VMEM((req_size, 4, rows, width), jnp.bfloat16),
            dma(tp_size), dma(tp_size), dma(tp_size), dma(tp_size), dma(tp_size), dma(tp_size),
            dma(req_size, 4), dma(req_size, 4),
        ],
        compiler_params=pltpu.CompilerParams(
            collective_id=1, has_side_effects=True, vmem_limit_bytes=40 << 20
        ),
    )(summed, stats, gated, mixer_gain[None], mamba_out, attention_out, residual, final_gain[None])


def body(
    residual,
    cache_lengths,
    input_gain,
    inner_weight,
    step_weight,
    step_bias,
    decay_log,
    skip_gain,
    conv_weight,
    conv_state,
    coupling_weight,
    coupling_conv,
    coupling_state,
    scan_state,
    mixer_gain,
    attention_weight,
    sink_cache,
    window_cache,
    mamba_out,
    attention_out,
    final_gain,
    output_head,
):
    row_count = residual.shape[0]
    tp_size = lax.axis_size("tp")
    tp_index = lax.axis_index("tp")
    local_units = inner_weight.shape[2]
    half_width = KVH * HD
    normed = norm_rows(residual, input_gain)
    projected = jnp.einsum(
        "rd,dtc->rtc", normed, inner_weight, preferred_element_type=jnp.float32
    ).astype(jnp.bfloat16)
    gate_rows = lax.optimization_barrier(projected[:, 0, :])
    x_rows, new_conv_state = conv_apply(conv_state, projected[:, 1, :], conv_weight)
    step_rows = lax.optimization_barrier(
        jnp.dot(normed, step_weight, preferred_element_type=jnp.float32).astype(jnp.bfloat16)
    )
    step_size = jax.nn.softplus(step_rows.astype(jnp.float32) + step_bias)
    decay_rate = jnp.exp(-step_size * jnp.exp(decay_log))
    coupling_pre = jnp.dot(normed, coupling_weight, preferred_element_type=jnp.float32).astype(
        jnp.bfloat16
    )
    coupling_rows, new_coupling_state = conv_apply(coupling_state, coupling_pre, coupling_conv)
    qkv_local = jnp.dot(normed, attention_weight, preferred_element_type=jnp.float32).astype(
        jnp.bfloat16
    )
    qkv_rows, coupling_all = (
        lax.all_gather(qkv_local, "tp", axis=1, tiled=True),
        lax.all_gather(coupling_rows.astype(jnp.bfloat16), "tp", axis=1, tiled=True),
    )
    new_key_value = qkv_rows[:, QH * HD :]
    window_slots = window_cache.shape[1]
    slot_index = tp_index * window_slots + jnp.arange(window_slots, dtype=jnp.int32)
    length_column = cache_lengths[:, None]
    back_steps = (length_column - 1 - slot_index[None, :]) % WIN
    position = length_column - 1 - back_steps
    live_mask = (position >= SINK) & (back_steps != WIN - 1)
    extra_live = (jnp.arange(128) < SINK + 1) & (tp_index == 0)
    mask = jnp.concatenate(
        [live_mask, jnp.broadcast_to(extra_live, (row_count, 128))], axis=1
    ).astype(jnp.float32)
    extra = jnp.concatenate(
        [
            sink_cache,
            new_key_value[:, None, :],
            jnp.zeros((row_count, EXTRA - SINK - 1, 2 * half_width), jnp.bfloat16),
        ],
        axis=1,
    )
    spread = lambda per_head: jnp.repeat(per_head, MP, axis=-1)
    new_state, summed, stats, gated = mixer(
        qkv_rows, extra, mask, window_cache, scan_state.reshape(row_count, local_units, NS),
        coupling_all, x_rows, spread(step_size), spread(decay_rate), gate_rows,
        spread(skip_gain)[None], tp_size,
    )
    new_scan_state = new_state.reshape(scan_state.shape)
    new_residual, final_rows = joint(
        summed, stats, gated, mixer_gain, mamba_out, attention_out, residual, final_gain
    )
    vocab_logits = jnp.dot(
        final_rows,
        output_head,
        preferred_element_type=jnp.float32,
    )
    logits = lax.all_to_all(
        vocab_logits.astype(jnp.bfloat16), ("req", "tp"), split_axis=0, concat_axis=1, tiled=True
    ).astype(vocab_logits.dtype)
    return (new_residual, logits, new_scan_state, new_conv_state, new_coupling_state, new_key_value)


def solution(mesh):
    return jax.shard_map(
        body,
        mesh=mesh,
        in_specs=(
            P("req", None),
            P("req"),
            P(),
            P(None, None, "tp"),
            P(None, "tp"),
            P("tp"),
            P("tp"),
            P("tp"),
            P(None, "tp"),
            P("req", None, "tp"),
            P(None, "tp"),
            P(None, "tp"),
            P("req", None, "tp"),
            P("req", "tp", None, None),
            P("tp"),
            P(None, "tp"),
            P("req", None, None),
            P("req", "tp", None),
            P("tp", None),
            P("tp", None),
            P(),
            P(None, ("req", "tp")),
        ),
        out_specs=(
            P("req", "tp"),
            P(("req", "tp"), None),
            P("req", "tp", None, None),
            P("req", None, "tp"),
            P("req", None, "tp"),
            P("req", None),
        ),
        check_vma=False,
    )
```

```python
import functools

import jax
import jax.numpy as jnp
from jax import lax
from jax.experimental import pallas as pl
from jax.experimental.pallas import tpu as pltpu
from jax.sharding import PartitionSpec as P

MH = 24
MP = 64
NS = 256
QH = 8
KVH = 2
HD = 128
WIN = 1024
SINK = 4
BR = 8
EXTRA = 16

EPSILON = 1e-05
NEG_BIG = -1e30
MESH = pl.DeviceIdType.MESH
NT = (((1,), (1,)), ((), ()))


def norm_rows(values, gain):
    widened = values.astype(jnp.float32)
    mean_sq = jnp.mean(widened * widened, axis=-1, keepdims=True)
    return (widened * lax.rsqrt(mean_sq + EPSILON) * gain).astype(jnp.bfloat16)


def silu(v):
    return v / (1.0 + jnp.exp(-v))


def conv_rows(state_ref, fresh, taps_ref):
    steps = [state_ref[k].astype(jnp.float32) for k in range(3)] + [fresh.astype(jnp.float32)]
    taps = taps_ref[...].astype(jnp.float32)
    mixed = steps[0] * taps[0:1]
    for k in range(1, 4):
        mixed = mixed + steps[k] * taps[k : k + 1]
    return silu(mixed)


def by_head(ref, g, shape):
    lane = lax.broadcasted_iota(jnp.int32, shape, 1)
    return jnp.where(lane < MP, ref[2 * g], ref[2 * g + 1])


def entry_kernel(
    tp_size, bias_ref, log_ref, residual_ref, gain_ref, attention_ref, coupling_ref, taps_ref,
    state_ref, step_weight_ref, normed_ref, pre_ref, qkv_ref, coup_ref, step_ref, decay_ref,
    qkv_s, qkv_r, coup_s, coup_r,
):
    r = lax.axis_index("req")
    t = lax.axis_index("tp")
    peers = [lax.rem(t + k, tp_size) for k in range(tp_size)]
    barrier = pltpu.get_barrier_semaphore()
    for k in range(1, tp_size):
        pl.semaphore_signal(barrier, inc=1, device_id=(r, peers[k]), device_id_type=MESH)
    normed = norm_rows(residual_ref[...], gain_ref[...])
    normed_ref[...] = normed
    copies = []

    def share(out_ref, value, ssem, rsem):
        width = value.shape[1]
        cols = pl.ds(pl.multiple_of(t * width, 128), width)
        out_ref[:, cols] = value
        for k in range(1, tp_size):
            copy = pltpu.make_async_remote_copy(
                src_ref=out_ref.at[:, cols], dst_ref=out_ref.at[:, cols], send_sem=ssem.at[k],
                recv_sem=rsem.at[k], device_id=(r, peers[k]), device_id_type=MESH,
            )
            copy.start()
            copies.append(copy)

    qkv = jnp.dot(normed, attention_ref[...], preferred_element_type=jnp.float32)
    pl.semaphore_wait(barrier, tp_size - 1)
    share(qkv_ref, qkv.astype(jnp.bfloat16), qkv_s, qkv_r)
    pre = jnp.dot(normed, coupling_ref[...], preferred_element_type=jnp.float32).astype(jnp.bfloat16)
    pre_ref[...] = pre
    share(coup_ref, conv_rows(state_ref, pre, taps_ref).astype(jnp.bfloat16), coup_s, coup_r)
    steps = (
        lax.dot_general(normed, step_weight_ref[...], NT, preferred_element_type=jnp.float32)
        .astype(jnp.bfloat16)
        .astype(jnp.float32)
    )
    shape = (normed.shape[0], 2 * MP)
    for g in range(steps.shape[1] // 2):
        lane = lax.broadcasted_iota(jnp.int32, shape, 1)
        v = jnp.where(lane < MP, steps[:, 2 * g : 2 * g + 1], steps[:, 2 * g + 1 : 2 * g + 2])
        v = v + by_head(bias_ref, g, shape)
        size = jnp.maximum(v, 0.0) + jnp.log1p(jnp.exp(-jnp.abs(v)))
        step_ref[:, g * 2 * MP : (g + 1) * 2 * MP] = size
        decay_ref[:, g * 2 * MP : (g + 1) * 2 * MP] = jnp.exp(
            -size * jnp.exp(by_head(log_ref, g, shape))
        )
    for copy in copies:
        copy.wait()


def entry(bias, decay_log, residual, gain, attention_weight, coupling_weight, taps, state, step_weight):
    tp_size = lax.axis_size("tp")
    rows, model = residual.shape
    units = bias.shape[0] * MP
    vmem = pl.BlockSpec(memory_space=pltpu.VMEM)
    smem = pl.BlockSpec(memory_space=pltpu.SMEM)
    dma = pltpu.SemaphoreType.DMA((tp_size,))
    shaped = jax.ShapeDtypeStruct
    return pl.pallas_call(
        functools.partial(entry_kernel, tp_size),
        in_specs=[smem] * 2 + [vmem] * 7,
        out_specs=[vmem] * 6,
        out_shape=[
            shaped((rows, model), jnp.bfloat16),
            shaped((rows, coupling_weight.shape[1]), jnp.bfloat16),
            shaped((rows, attention_weight.shape[1] * tp_size), jnp.bfloat16),
            shaped((rows, coupling_weight.shape[1] * tp_size), jnp.bfloat16),
            shaped((rows, units), jnp.float32),
            shaped((rows, units), jnp.float32),
        ],
        scratch_shapes=[dma] * 4,
        compiler_params=pltpu.CompilerParams(
            collective_id=0, has_side_effects=True, vmem_limit_bytes=16 << 20
        ),
    )(bias, decay_log, residual, gain[None], attention_weight, coupling_weight, taps, state, step_weight)


def mixer_kernel(
    len_ref, skip_ref, qkv_ref, sink_ref, window_ref, state_ref, coup_ref, pre_ref, coup_state_ref,
    projected_ref, taps_ref, conv_state_ref, step_ref, decay_ref, new_state_ref, new_conv_ref,
    new_coup_ref, summed_ref, stats_ref, gated_ref, heads_scr, extra_scr,
):
    half = KVH * HD
    group = QH // KVH
    t = lax.axis_index("tp")
    for h in range(QH):
        heads_scr[pl.ds(h, BR, stride=QH), :] = qkv_ref[:, h * HD : (h + 1) * HD].astype(jnp.float32)
    extra_scr[...] = jnp.zeros_like(extra_scr)
    fresh_rows = qkv_ref[:, QH * HD :].astype(jnp.float32)
    units = step_ref.shape[1]
    gate = projected_ref[0].astype(jnp.float32)
    x_pre = projected_ref[1]
    x = conv_rows(conv_state_ref, x_pre, taps_ref)
    new_conv_ref[0] = conv_state_ref[1]
    new_conv_ref[1] = conv_state_ref[2]
    new_conv_ref[2] = x_pre
    new_coup_ref[0] = coup_state_ref[1]
    new_coup_ref[1] = coup_state_ref[2]
    new_coup_ref[2] = pre_ref[...]
    head_row = lax.broadcasted_iota(jnp.int32, (QH, HD), 0)
    lane = lax.broadcasted_iota(jnp.int32, (QH, HD), 1)
    first_half = head_row < group
    step_x = step_ref[...] * x
    decay = decay_ref[...]
    step_x_t = step_x.T
    decay_t = decay.T
    coup = coup_ref[...]
    out_rows = coup[:, NS:]
    in_f32 = coup[:, :NS].astype(jnp.float32)
    both = jnp.sum(in_f32 * out_rows.astype(jnp.float32), axis=1, keepdims=True)
    read_rows = []
    for j in range(BR):
        q = heads_scr[j * QH : (j + 1) * QH, :]
        wide = jnp.concatenate(
            [jnp.where(first_half, q, 0.0), jnp.where(first_half, 0.0, q)], axis=1
        ).astype(jnp.bfloat16)
        extra_scr[j, :SINK, :] = sink_ref[j].astype(jnp.float32)
        extra_scr[j, SINK : SINK + 1, :] = fresh_rows[j : j + 1, :]
        extra = extra_scr[j].astype(jnp.bfloat16)
        s1 = lax.dot_general(
            wide, window_ref[j, :, :half], NT, preferred_element_type=jnp.float32
        ) * HD ** (-0.5)
        s2 = lax.dot_general(
            wide, extra[:, :half], NT, preferred_element_type=jnp.float32
        ) * HD ** (-0.5)
        last = len_ref[pl.program_id(0) * BR + j] - 1
        slots = window_ref.shape[1]
        slot = t * slots + lax.broadcasted_iota(jnp.int32, s1.shape, 1)
        back = jnp.bitwise_and(last - slot, WIN - 1)
        live1 = (last - back >= SINK) & (back != WIN - 1)
        live2 = lax.broadcasted_iota(jnp.int32, s2.shape, 1) < jnp.where(t == 0, SINK + 1, 0)
        s1 = jnp.where(live1, s1, NEG_BIG)
        s2 = jnp.where(live2, s2, NEG_BIG)
        peak = jnp.maximum(
            jnp.max(s1, axis=1, keepdims=True), jnp.max(s2, axis=1, keepdims=True)
        )
        w1 = jnp.where(live1, jnp.exp(s1 - peak), 0.0)
        w2 = jnp.where(live2, jnp.exp(s2 - peak), 0.0)
        total = jnp.sum(w1, axis=1, keepdims=True) + jnp.sum(w2, axis=1, keepdims=True)
        acc = jnp.dot(
            w1.astype(jnp.bfloat16), window_ref[j, :, half:], preferred_element_type=jnp.float32
        ) + jnp.dot(
            w2.astype(jnp.bfloat16), extra[:, half:], preferred_element_type=jnp.float32
        )
        heads_scr[j * QH : (j + 1) * QH, :] = jnp.where(first_half, acc[:, :HD], acc[:, HD:])
        stats_ref[j : j + 1, :] = jnp.sum(
            jnp.where(lane == head_row, peak, 0.0)
            + jnp.where(lane == head_row + QH, total, 0.0),
            axis=0,
            keepdims=True,
        )
        state = state_ref[j]
        read_rows.append(
            lax.dot_general(out_rows, state, NT, preferred_element_type=jnp.float32)[j : j + 1, :]
        )
        new_state_ref[j] = (
            decay_t[:, j : j + 1] * state.astype(jnp.float32)
            + step_x_t[:, j : j + 1] * in_f32[j : j + 1, :]
        ).astype(jnp.bfloat16)
    per_chunk = summed_ref.shape[2] // HD
    for h in range(QH):
        summed_ref[h // per_chunk, :, (h % per_chunk) * HD : (h % per_chunk + 1) * HD] = heads_scr[
            pl.ds(h, BR, stride=QH), :
        ].astype(jnp.bfloat16)
    readout = decay * jnp.concatenate(read_rows, axis=0) + step_x * both
    skip = jnp.concatenate(
        [by_head(skip_ref, g, (BR, 2 * MP)) for g in range(units // (2 * MP))], axis=1
    )
    gated = (readout + skip * x) * silu(gate)
    gated_ref[...] = gated
    square = jnp.sum(gated * gated, axis=1, keepdims=True)
    stats_ref[...] = jnp.where(
        lax.broadcasted_iota(jnp.int32, stats_ref.shape, 1) == 2 * QH, square, stats_ref[...]
    )


def mixer(
    lengths, skip, qkv, sink, window, state, coup, pre, coup_state, projected, taps, conv_state,
    step, decay, tp_size,
):
    rows, units = step.shape
    row = lambda a: pl.BlockSpec((BR, a.shape[1]), lambda i: (i, 0))
    cube = lambda a: pl.BlockSpec((BR,) + a.shape[1:], lambda i: (i, 0, 0))
    steps = lambda a: pl.BlockSpec((3, BR, a.shape[2]), lambda i: (0, i, 0))
    smem = pl.BlockSpec(memory_space=pltpu.SMEM)
    chunk = QH * HD // tp_size
    return pl.pallas_call(
        mixer_kernel,
        grid=(rows // BR,),
        in_specs=[
            smem, smem, row(qkv), cube(sink), cube(window), cube(state), row(coup), row(pre),
            steps(coup_state), pl.BlockSpec((2, BR, units), lambda i: (0, i, 0)), pl.BlockSpec(taps.shape, lambda i: (0, 0)),
            steps(conv_state), row(step), row(decay),
        ],
        out_specs=[
            cube(state), steps(conv_state), steps(coup_state),
            pl.BlockSpec((tp_size, BR, chunk), lambda i: (0, i, 0)),
            pl.BlockSpec((BR, 128), lambda i: (i, 0)), row(step),
        ],
        out_shape=[
            jax.ShapeDtypeStruct(state.shape, jnp.bfloat16),
            jax.ShapeDtypeStruct(conv_state.shape, jnp.bfloat16),
            jax.ShapeDtypeStruct(coup_state.shape, jnp.bfloat16),
            jax.ShapeDtypeStruct((tp_size, rows, chunk), jnp.bfloat16),
            jax.ShapeDtypeStruct((rows, 128), jnp.float32),
            jax.ShapeDtypeStruct((rows, units), jnp.float32),
        ],
        scratch_shapes=[
            pltpu.VMEM((BR * QH, HD), jnp.float32),
            pltpu.VMEM((BR, EXTRA, 2 * KVH * HD), jnp.float32),
        ],
        compiler_params=pltpu.CompilerParams(vmem_limit_bytes=40 << 20),
    )(
        lengths, skip, qkv, sink, window, state, coup, pre, coup_state, projected, taps, conv_state,
        step, decay,
    )


def joint_kernel(
    tp_size, req_size, summed_ref, stats_ref, gated_ref, mixer_gain_ref, mamba_out_ref,
    attention_out_ref, residual_ref, final_gain_ref, new_residual_ref, final_ref,
    sum_buf, stat_buf, part_out, part_buf, gather, sum_s, sum_r, stat_s, stat_r, part_s, part_r,
    gat_s, gat_r,
):
    r = lax.axis_index("req")
    t = lax.axis_index("tp")
    rows = gated_ref.shape[0]
    width = new_residual_ref.shape[1]
    peers = [lax.rem(t + k, tp_size) for k in range(tp_size)]
    reqs = [lax.rem(r + k, req_size) for k in range(req_size)]
    barrier = pltpu.get_barrier_semaphore()
    for k in range(1, tp_size):
        pl.semaphore_signal(barrier, inc=1, device_id=(r, peers[k]), device_id_type=MESH)
    for k in range(1, req_size):
        pl.semaphore_signal(barrier, inc=1, device_id=(reqs[k], t), device_id_type=MESH)
    pl.semaphore_wait(barrier, tp_size - 1 + req_size - 1)

    def send(src, dst, ssem, rsem, where):
        copy = pltpu.make_async_remote_copy(
            src_ref=src, dst_ref=dst, send_sem=ssem, recv_sem=rsem,
            device_id=where, device_id_type=MESH,
        )
        copy.start()
        return copy

    first = []
    for k in range(1, tp_size):
        where = (r, peers[k])
        first.append(send(stats_ref, stat_buf.at[k], stat_s.at[k], stat_r.at[k], where))
        first.append(send(summed_ref.at[peers[k]], sum_buf.at[k], sum_s.at[k], sum_r.at[k], where))
    for copy in first:
        copy.wait()
    stats = [stats_ref[...]] + [stat_buf[k] for k in range(1, tp_size)]
    sums = [summed_ref[t].astype(jnp.float32)] + [
        sum_buf[k].astype(jnp.float32) for k in range(1, tp_size)
    ]
    lane = lax.broadcasted_iota(jnp.int32, (rows, 128), 1)
    local_heads = QH // tp_size
    pieces = []
    for hl in range(local_heads):
        h = t * local_heads + hl
        peaks = [jnp.sum(jnp.where(lane == h, s, 0.0), axis=1, keepdims=True) for s in stats]
        totals = [jnp.sum(jnp.where(lane == h + QH, s, 0.0), axis=1, keepdims=True) for s in stats]
        top = functools.reduce(jnp.maximum, peaks)
        scales = [jnp.exp(p - top) for p in peaks]
        below = functools.reduce(jnp.add, [a * b for a, b in zip(scales, totals)])
        above = functools.reduce(
            jnp.add, [a * b[:, hl * HD : (hl + 1) * HD] for a, b in zip(scales, sums)]
        )
        pieces.append((above / below).astype(jnp.bfloat16))
    attended = jnp.concatenate(pieces, axis=1)
    square = functools.reduce(jnp.add, [s[:, 2 * QH : 2 * QH + 1] for s in stats])
    mamba = (
        gated_ref[...] * lax.rsqrt(square / (MH * MP) + EPSILON) * mixer_gain_ref[...]
    ).astype(jnp.bfloat16)

    def partial(p):
        cols = pl.ds(pl.multiple_of(p * width, 128), width)
        return jnp.dot(mamba, mamba_out_ref[:, cols], preferred_element_type=jnp.float32) + jnp.dot(
            attended, attention_out_ref[:, cols], preferred_element_type=jnp.float32
        )

    second = []
    for k in range(1, tp_size):
        part_out[k] = partial(peers[k]).astype(jnp.bfloat16)
        second.append(
            send(part_out.at[k], part_buf.at[k], part_s.at[k], part_r.at[k], (r, peers[k]))
        )
    mixed = partial(t)
    for k in range(1, tp_size):
        second[k - 1].wait()
        mixed = mixed + part_buf[k].astype(jnp.float32)
    own = pl.ds(pl.multiple_of(t * width, 128), width)
    fresh = (residual_ref[:, own].astype(jnp.float32) + mixed).astype(jnp.bfloat16)
    new_residual_ref[...] = fresh
    gather[0, 0] = fresh

    beside = t + 1 - 2 * lax.rem(t, 2)
    across = lax.rem(t + 2, tp_size)
    owner = [t, beside, across, lax.rem(beside + 2, tp_size)]
    along = [None]
    for k in range(1, req_size):
        along.append(
            send(gather.at[0, 0], gather.at[k, 0], gat_s.at[k, 0], gat_r.at[k, 0], (reqs[k], t))
        )
    over, near, far = [], [], []
    for k in range(req_size):
        if k:
            along[k].wait_recv()
        over.append(
            send(gather.at[k, 0], gather.at[k, 2], gat_s.at[k, 2], gat_r.at[k, 2], (r, across))
        )
        near.append(
            send(gather.at[k, 0], gather.at[k, 1], gat_s.at[k, 1], gat_r.at[k, 1], (r, beside))
        )
    for k in range(req_size):
        over[k].wait_recv()
        far.append(
            send(gather.at[k, 2], gather.at[k, 3], gat_s.at[k, 3], gat_r.at[k, 3], (r, beside))
        )
    for k in range(req_size):
        near[k].wait_recv()
        far[k].wait_recv()
        values = [gather[k, i].astype(jnp.float32) for i in range(4)]
        mean = functools.reduce(
            jnp.add, [jnp.sum(v * v, axis=1, keepdims=True) for v in values]
        ) / (width * tp_size)
        scale = lax.rsqrt(mean + EPSILON)
        source = lax.rem(r + req_size - k, req_size)
        at = pl.ds(pl.multiple_of(source * rows, rows), rows)
        for i in range(4):
            cols = pl.ds(pl.multiple_of(owner[i] * width, 128), width)
            final_ref[at, cols] = (values[i] * scale * final_gain_ref[:, cols]).astype(jnp.bfloat16)
    for k in range(req_size):
        if k:
            along[k].wait_send()
        over[k].wait_send()
        near[k].wait_send()
        far[k].wait_send()


def joint(summed, stats, gated, mixer_gain, mamba_out, attention_out, residual, final_gain):
    tp_size = lax.axis_size("tp")
    req_size = lax.axis_size("req")
    rows, model = residual.shape
    width = model // tp_size
    chunk = summed.shape[2]
    dma = lambda *shape: pltpu.SemaphoreType.DMA(shape)
    vmem = pl.BlockSpec(memory_space=pltpu.VMEM)
    return pl.pallas_call(
        functools.partial(joint_kernel, tp_size, req_size),
        in_specs=[vmem] * 8,
        out_specs=[vmem] * 2,
        out_shape=[
            jax.ShapeDtypeStruct((rows, width), jnp.bfloat16),
            jax.ShapeDtypeStruct((rows * req_size, model), jnp.bfloat16),
        ],
        scratch_shapes=[
            pltpu.VMEM((tp_size, rows, chunk), jnp.bfloat16),
            pltpu.VMEM((tp_size, rows, 128), jnp.float32),
            pltpu.VMEM((tp_size, rows, width), jnp.bfloat16),
            pltpu.VMEM((tp_size, rows, width), jnp.bfloat16),
            pltpu.VMEM((req_size, 4, rows, width), jnp.bfloat16),
            dma(tp_size), dma(tp_size), dma(tp_size), dma(tp_size), dma(tp_size), dma(tp_size),
            dma(req_size, 4), dma(req_size, 4),
        ],
        compiler_params=pltpu.CompilerParams(
            collective_id=1, has_side_effects=True, vmem_limit_bytes=40 << 20
        ),
    )(summed, stats, gated, mixer_gain[None], mamba_out, attention_out, residual, final_gain[None])


def body(
    residual,
    cache_lengths,
    input_gain,
    inner_weight,
    step_weight,
    step_bias,
    decay_log,
    skip_gain,
    conv_weight,
    conv_state,
    coupling_weight,
    coupling_conv,
    coupling_state,
    scan_state,
    mixer_gain,
    attention_weight,
    sink_cache,
    window_cache,
    mamba_out,
    attention_out,
    final_gain,
    output_head,
):
    row_count = residual.shape[0]
    tp_size = lax.axis_size("tp")
    local_units = inner_weight.shape[2]
    swap = lambda array: jnp.transpose(array, (1, 0, 2))
    coup_state = swap(coupling_state)
    normed, coupling_pre, qkv_rows, coupling_all, step_size, decay_rate = entry(
        step_bias, decay_log, residual, input_gain, attention_weight, coupling_weight,
        coupling_conv, coup_state, step_weight.T,
    )
    projected = jnp.einsum(
        "rd,dtc->trc", normed, inner_weight, preferred_element_type=jnp.float32
    ).astype(jnp.bfloat16)
    new_key_value = qkv_rows[:, QH * HD :]
    new_state, new_conv, new_coup, summed, stats, gated = mixer(
        cache_lengths, skip_gain, qkv_rows, sink_cache, window_cache,
        scan_state.reshape(row_count, local_units, NS), coupling_all, coupling_pre, coup_state,
        projected, conv_weight, swap(conv_state), step_size, decay_rate, tp_size,
    )
    new_conv_state = swap(new_conv)
    new_coupling_state = swap(new_coup)
    new_scan_state = new_state.reshape(scan_state.shape)
    new_residual, final_rows = joint(
        summed, stats, gated, mixer_gain, mamba_out, attention_out, residual, final_gain
    )
    vocab_logits = jnp.dot(
        final_rows,
        output_head,
        preferred_element_type=jnp.float32,
    )
    logits = lax.all_to_all(
        vocab_logits.astype(jnp.bfloat16), ("req", "tp"), split_axis=0, concat_axis=1, tiled=True
    ).astype(vocab_logits.dtype)
    return (new_residual, logits, new_scan_state, new_conv_state, new_coupling_state, new_key_value)


def solution(mesh):
    return jax.shard_map(
        body,
        mesh=mesh,
        in_specs=(
            P("req", None),
            P("req"),
            P(),
            P(None, None, "tp"),
            P(None, "tp"),
            P("tp"),
            P("tp"),
            P("tp"),
            P(None, "tp"),
            P("req", None, "tp"),
            P(None, "tp"),
            P(None, "tp"),
            P("req", None, "tp"),
            P("req", "tp", None, None),
            P("tp"),
            P(None, "tp"),
            P("req", None, None),
            P("req", "tp", None),
            P("tp", None),
            P("tp", None),
            P(),
            P(None, ("req", "tp")),
        ),
        out_specs=(
            P("req", "tp"),
            P(("req", "tp"), None),
            P("req", "tp", None, None),
            P("req", None, "tp"),
            P("req", None, "tp"),
            P("req", None),
        ),
        check_vma=False,
    )
```

```python
import functools

import jax
import jax.numpy as jnp
from jax import lax
from jax.experimental import pallas as pl
from jax.experimental.pallas import tpu as pltpu
from jax.sharding import PartitionSpec as P

MH = 24
MP = 64
NS = 256
QH = 8
KVH = 2
HD = 128
WIN = 1024
SINK = 4
BR = 8
EXTRA = 16

EPSILON = 1e-05
NEG_BIG = -1e30
MESH = pl.DeviceIdType.MESH
NT = (((1,), (1,)), ((), ()))


def norm_rows(values, gain):
    widened = values.astype(jnp.float32)
    mean_sq = jnp.mean(widened * widened, axis=-1, keepdims=True)
    return (widened * lax.rsqrt(mean_sq + EPSILON) * gain).astype(jnp.bfloat16)


def silu(v):
    return v / (1.0 + jnp.exp(-v))


def conv_rows(state_ref, fresh, taps_ref):
    steps = [state_ref[k].astype(jnp.float32) for k in range(3)] + [fresh.astype(jnp.float32)]
    taps = taps_ref[...].astype(jnp.float32)
    mixed = steps[0] * taps[0:1]
    for k in range(1, 4):
        mixed = mixed + steps[k] * taps[k : k + 1]
    return silu(mixed)


def by_head(ref, g, shape):
    lane = lax.broadcasted_iota(jnp.int32, shape, 1)
    return jnp.where(lane < MP, ref[2 * g], ref[2 * g + 1])


def entry_kernel(
    tp_size, bias_ref, log_ref, residual_ref, gain_ref, attention_ref, coupling_ref, taps_ref,
    state_ref, step_weight_ref, normed_ref, pre_ref, qkv_ref, coup_ref, step_ref, decay_ref,
    qkv_s, qkv_r, coup_s, coup_r,
):
    r = lax.axis_index("req")
    t = lax.axis_index("tp")
    peers = [lax.rem(t + k, tp_size) for k in range(tp_size)]
    barrier = pltpu.get_barrier_semaphore()
    for k in range(1, tp_size):
        pl.semaphore_signal(barrier, inc=1, device_id=(r, peers[k]), device_id_type=MESH)
    normed = norm_rows(residual_ref[...], gain_ref[...])
    normed_ref[...] = normed
    copies = []

    def share(out_ref, value, ssem, rsem):
        width = value.shape[1]
        cols = pl.ds(pl.multiple_of(t * width, 128), width)
        out_ref[:, cols] = value
        for k in range(1, tp_size):
            copy = pltpu.make_async_remote_copy(
                src_ref=out_ref.at[:, cols], dst_ref=out_ref.at[:, cols], send_sem=ssem.at[k],
                recv_sem=rsem.at[k], device_id=(r, peers[k]), device_id_type=MESH,
            )
            copy.start()
            copies.append(copy)

    qkv = jnp.dot(normed, attention_ref[...], preferred_element_type=jnp.float32)
    pl.semaphore_wait(barrier, tp_size - 1)
    share(qkv_ref, qkv.astype(jnp.bfloat16), qkv_s, qkv_r)
    pre = jnp.dot(normed, coupling_ref[...], preferred_element_type=jnp.float32).astype(jnp.bfloat16)
    pre_ref[...] = pre
    share(coup_ref, conv_rows(state_ref, pre, taps_ref).astype(jnp.bfloat16), coup_s, coup_r)
    steps = (
        lax.dot_general(normed, step_weight_ref[...], NT, preferred_element_type=jnp.float32)
        .astype(jnp.bfloat16)
        .astype(jnp.float32)
    )
    shape = (normed.shape[0], 2 * MP)
    for g in range(steps.shape[1] // 2):
        lane = lax.broadcasted_iota(jnp.int32, shape, 1)
        v = jnp.where(lane < MP, steps[:, 2 * g : 2 * g + 1], steps[:, 2 * g + 1 : 2 * g + 2])
        v = v + by_head(bias_ref, g, shape)
        size = jnp.maximum(v, 0.0) + jnp.log1p(jnp.exp(-jnp.abs(v)))
        step_ref[:, g * 2 * MP : (g + 1) * 2 * MP] = size
        decay_ref[:, g * 2 * MP : (g + 1) * 2 * MP] = jnp.exp(
            -size * jnp.exp(by_head(log_ref, g, shape))
        )
    for copy in copies:
        copy.wait()


def entry(bias, decay_log, residual, gain, attention_weight, coupling_weight, taps, state, step_weight):
    tp_size = lax.axis_size("tp")
    rows, model = residual.shape
    units = bias.shape[0] * MP
    vmem = pl.BlockSpec(memory_space=pltpu.VMEM)
    smem = pl.BlockSpec(memory_space=pltpu.SMEM)
    dma = pltpu.SemaphoreType.DMA((tp_size,))
    shaped = jax.ShapeDtypeStruct
    return pl.pallas_call(
        functools.partial(entry_kernel, tp_size),
        in_specs=[smem] * 2 + [vmem] * 7,
        out_specs=[vmem] * 6,
        out_shape=[
            shaped((rows, model), jnp.bfloat16),
            shaped((rows, coupling_weight.shape[1]), jnp.bfloat16),
            shaped((rows, attention_weight.shape[1] * tp_size), jnp.bfloat16),
            shaped((rows, coupling_weight.shape[1] * tp_size), jnp.bfloat16),
            shaped((rows, units), jnp.float32),
            shaped((rows, units), jnp.float32),
        ],
        scratch_shapes=[dma] * 4,
        compiler_params=pltpu.CompilerParams(
            collective_id=0, has_side_effects=True, vmem_limit_bytes=16 << 20
        ),
    )(bias, decay_log, residual, gain[None], attention_weight, coupling_weight, taps, state, step_weight)


def mixer_kernel(
    len_ref, skip_ref, qkv_ref, sink_ref, window_ref, state_ref, coup_ref, pre_ref, coup_state_ref,
    projected_ref, taps_ref, conv_state_ref, step_ref, decay_ref, new_state_ref, new_conv_ref,
    new_coup_ref, summed_ref, stats_ref, gated_ref, heads_scr, extra_scr,
):
    half = KVH * HD
    group = QH // KVH
    t = lax.axis_index("tp")
    for h in range(QH):
        heads_scr[pl.ds(h, BR, stride=QH), :] = qkv_ref[:, h * HD : (h + 1) * HD].astype(jnp.float32)
    extra_scr[...] = jnp.zeros_like(extra_scr)
    fresh_rows = qkv_ref[:, QH * HD :].astype(jnp.float32)
    units = step_ref.shape[1]
    gate = projected_ref[0].astype(jnp.float32)
    x_pre = projected_ref[1]
    x = conv_rows(conv_state_ref, x_pre, taps_ref)
    new_conv_ref[0] = conv_state_ref[1]
    new_conv_ref[1] = conv_state_ref[2]
    new_conv_ref[2] = x_pre
    new_coup_ref[0] = coup_state_ref[1]
    new_coup_ref[1] = coup_state_ref[2]
    new_coup_ref[2] = pre_ref[...]
    head_row = lax.broadcasted_iota(jnp.int32, (QH, HD), 0)
    lane = lax.broadcasted_iota(jnp.int32, (QH, HD), 1)
    first_half = head_row < group
    step_x = step_ref[...] * x
    decay = decay_ref[...]
    step_x_t = step_x.T
    decay_t = decay.T
    coup = coup_ref[...]
    out_rows = coup[:, NS:]
    in_f32 = coup[:, :NS].astype(jnp.float32)
    both = jnp.sum(in_f32 * out_rows.astype(jnp.float32), axis=1, keepdims=True)
    read_rows = []
    for j in range(BR):
        q = heads_scr[j * QH : (j + 1) * QH, :]
        wide = jnp.concatenate(
            [jnp.where(first_half, q, 0.0), jnp.where(first_half, 0.0, q)], axis=1
        ).astype(jnp.bfloat16)
        extra_scr[j, :SINK, :] = sink_ref[j].astype(jnp.float32)
        extra_scr[j, SINK : SINK + 1, :] = fresh_rows[j : j + 1, :]
        extra = extra_scr[j].astype(jnp.bfloat16)
        s1 = lax.dot_general(
            wide, window_ref[j, :, :half], NT, preferred_element_type=jnp.float32
        ) * HD ** (-0.5)
        s2 = lax.dot_general(
            wide, extra[:, :half], NT, preferred_element_type=jnp.float32
        ) * HD ** (-0.5)
        last = len_ref[pl.program_id(0) * BR + j] - 1
        slots = window_ref.shape[1]
        slot = t * slots + lax.broadcasted_iota(jnp.int32, s1.shape, 1)
        back = jnp.bitwise_and(last - slot, WIN - 1)
        live1 = (last - back >= SINK) & (back != WIN - 1)
        live2 = lax.broadcasted_iota(jnp.int32, s2.shape, 1) < jnp.where(t == 0, SINK + 1, 0)
        s1 = jnp.where(live1, s1, NEG_BIG)
        s2 = jnp.where(live2, s2, NEG_BIG)
        peak = jnp.maximum(
            jnp.max(s1, axis=1, keepdims=True), jnp.max(s2, axis=1, keepdims=True)
        )
        w1 = jnp.where(live1, jnp.exp(s1 - peak), 0.0)
        w2 = jnp.where(live2, jnp.exp(s2 - peak), 0.0)
        total = jnp.sum(w1, axis=1, keepdims=True) + jnp.sum(w2, axis=1, keepdims=True)
        acc = jnp.dot(
            w1.astype(jnp.bfloat16), window_ref[j, :, half:], preferred_element_type=jnp.float32
        ) + jnp.dot(
            w2.astype(jnp.bfloat16), extra[:, half:], preferred_element_type=jnp.float32
        )
        heads_scr[j * QH : (j + 1) * QH, :] = jnp.where(first_half, acc[:, :HD], acc[:, HD:])
        stats_ref[j : j + 1, :] = jnp.sum(
            jnp.where(lane == head_row, peak, 0.0)
            + jnp.where(lane == head_row + QH, total, 0.0),
            axis=0,
            keepdims=True,
        )
        state = state_ref[j]
        read_rows.append(
            lax.dot_general(out_rows, state, NT, preferred_element_type=jnp.float32)[j : j + 1, :]
        )
        new_state_ref[j] = (
            decay_t[:, j : j + 1] * state.astype(jnp.float32)
            + step_x_t[:, j : j + 1] * in_f32[j : j + 1, :]
        ).astype(jnp.bfloat16)
    per_chunk = summed_ref.shape[2] // HD
    for h in range(QH):
        summed_ref[h // per_chunk, :, (h % per_chunk) * HD : (h % per_chunk + 1) * HD] = heads_scr[
            pl.ds(h, BR, stride=QH), :
        ].astype(jnp.bfloat16)
    readout = decay * jnp.concatenate(read_rows, axis=0) + step_x * both
    skip = jnp.concatenate(
        [by_head(skip_ref, g, (BR, 2 * MP)) for g in range(units // (2 * MP))], axis=1
    )
    gated = (readout + skip * x) * silu(gate)
    gated_ref[...] = gated
    square = jnp.sum(gated * gated, axis=1, keepdims=True)
    stats_ref[...] = jnp.where(
        lax.broadcasted_iota(jnp.int32, stats_ref.shape, 1) == 2 * QH, square, stats_ref[...]
    )


def mixer(
    lengths, skip, qkv, sink, window, state, coup, pre, coup_state, projected, taps, conv_state,
    step, decay, tp_size,
):
    rows, units = step.shape
    row = lambda a: pl.BlockSpec((BR, a.shape[1]), lambda i: (i, 0))
    cube = lambda a: pl.BlockSpec((BR,) + a.shape[1:], lambda i: (i, 0, 0))
    steps = lambda a: pl.BlockSpec((3, BR, a.shape[2]), lambda i: (0, i, 0))
    smem = pl.BlockSpec(memory_space=pltpu.SMEM)
    chunk = QH * HD // tp_size
    return pl.pallas_call(
        mixer_kernel,
        grid=(rows // BR,),
        in_specs=[
            smem, smem, row(qkv), cube(sink), cube(window), cube(state), row(coup), row(pre),
            steps(coup_state), pl.BlockSpec((2, BR, units), lambda i: (0, i, 0)), pl.BlockSpec(taps.shape, lambda i: (0, 0)),
            steps(conv_state), row(step), row(decay),
        ],
        out_specs=[
            cube(state), steps(conv_state), steps(coup_state),
            pl.BlockSpec((tp_size, BR, chunk), lambda i: (0, i, 0)),
            pl.BlockSpec((BR, 128), lambda i: (i, 0)), row(step),
        ],
        out_shape=[
            jax.ShapeDtypeStruct(state.shape, jnp.bfloat16),
            jax.ShapeDtypeStruct(conv_state.shape, jnp.bfloat16),
            jax.ShapeDtypeStruct(coup_state.shape, jnp.bfloat16),
            jax.ShapeDtypeStruct((tp_size, rows, chunk), jnp.bfloat16),
            jax.ShapeDtypeStruct((rows, 128), jnp.float32),
            jax.ShapeDtypeStruct((rows, units), jnp.float32),
        ],
        scratch_shapes=[
            pltpu.VMEM((BR * QH, HD), jnp.float32),
            pltpu.VMEM((BR, EXTRA, 2 * KVH * HD), jnp.float32),
        ],
        compiler_params=pltpu.CompilerParams(vmem_limit_bytes=40 << 20),
    )(
        lengths, skip, qkv, sink, window, state, coup, pre, coup_state, projected, taps, conv_state,
        step, decay,
    )


def joint_kernel(
    tp_size, req_size, summed_ref, stats_ref, gated_ref, mixer_gain_ref, mamba_out_ref,
    attention_out_ref, residual_ref, final_gain_ref, head_ref, new_residual_ref, logits_ref,
    sum_buf, stat_buf, part_out, part_buf, gather, final_buf, head_buf, logit_out, logit_buf,
    sum_s, sum_r, stat_s, stat_r, part_s, part_r, gat_s, gat_r, log_s, log_r, head_sem,
):
    r = lax.axis_index("req")
    t = lax.axis_index("tp")
    rows = gated_ref.shape[0]
    width = new_residual_ref.shape[1]
    peers = [lax.rem(t + k, tp_size) for k in range(tp_size)]
    reqs = [lax.rem(r + k, req_size) for k in range(req_size)]
    barrier = pltpu.get_barrier_semaphore()
    load_head = pltpu.make_async_copy(head_ref, head_buf, head_sem.at[0])
    load_head.start()
    for k in range(req_size):
        for q in range(tp_size):
            if k or q:
                pl.semaphore_signal(
                    barrier, inc=1, device_id=(reqs[k], peers[q]), device_id_type=MESH
                )
    pl.semaphore_wait(barrier, tp_size * req_size - 1)

    def send(src, dst, ssem, rsem, where):
        copy = pltpu.make_async_remote_copy(
            src_ref=src, dst_ref=dst, send_sem=ssem, recv_sem=rsem,
            device_id=where, device_id_type=MESH,
        )
        copy.start()
        return copy

    first = []
    for k in range(1, tp_size):
        where = (r, peers[k])
        first.append(send(stats_ref, stat_buf.at[k], stat_s.at[k], stat_r.at[k], where))
        first.append(send(summed_ref.at[peers[k]], sum_buf.at[k], sum_s.at[k], sum_r.at[k], where))
    for copy in first:
        copy.wait()
    stats = [stats_ref[...]] + [stat_buf[k] for k in range(1, tp_size)]
    sums = [summed_ref[t].astype(jnp.float32)] + [
        sum_buf[k].astype(jnp.float32) for k in range(1, tp_size)
    ]
    lane = lax.broadcasted_iota(jnp.int32, (rows, 128), 1)
    local_heads = QH // tp_size
    pieces = []
    for hl in range(local_heads):
        h = t * local_heads + hl
        peaks = [jnp.sum(jnp.where(lane == h, s, 0.0), axis=1, keepdims=True) for s in stats]
        totals = [jnp.sum(jnp.where(lane == h + QH, s, 0.0), axis=1, keepdims=True) for s in stats]
        top = functools.reduce(jnp.maximum, peaks)
        scales = [jnp.exp(p - top) for p in peaks]
        below = functools.reduce(jnp.add, [a * b for a, b in zip(scales, totals)])
        above = functools.reduce(
            jnp.add, [a * b[:, hl * HD : (hl + 1) * HD] for a, b in zip(scales, sums)]
        )
        pieces.append((above / below).astype(jnp.bfloat16))
    attended = jnp.concatenate(pieces, axis=1)
    square = functools.reduce(jnp.add, [s[:, 2 * QH : 2 * QH + 1] for s in stats])
    mamba = (
        gated_ref[...] * lax.rsqrt(square / (MH * MP) + EPSILON) * mixer_gain_ref[...]
    ).astype(jnp.bfloat16)

    def partial(p):
        cols = pl.ds(pl.multiple_of(p * width, 128), width)
        return jnp.dot(mamba, mamba_out_ref[:, cols], preferred_element_type=jnp.float32) + jnp.dot(
            attended, attention_out_ref[:, cols], preferred_element_type=jnp.float32
        )

    second = []
    for k in range(1, tp_size):
        part_out[k] = partial(peers[k]).astype(jnp.bfloat16)
        second.append(
            send(part_out.at[k], part_buf.at[k], part_s.at[k], part_r.at[k], (r, peers[k]))
        )
    mixed = partial(t)
    for k in range(1, tp_size):
        second[k - 1].wait()
        mixed = mixed + part_buf[k].astype(jnp.float32)
    own = pl.ds(pl.multiple_of(t * width, 128), width)
    fresh = (residual_ref[:, own].astype(jnp.float32) + mixed).astype(jnp.bfloat16)
    new_residual_ref[...] = fresh
    gather[0, 0] = fresh

    beside = t + 1 - 2 * lax.rem(t, 2)
    across = lax.rem(t + 2, tp_size)
    owner = [t, beside, across, lax.rem(beside + 2, tp_size)]
    along = [None]
    for k in range(1, req_size):
        along.append(
            send(gather.at[0, 0], gather.at[k, 0], gat_s.at[k, 0], gat_r.at[k, 0], (reqs[k], t))
        )
    over, near, far = [], [], []
    for k in range(req_size):
        if k:
            along[k].wait_recv()
        over.append(
            send(gather.at[k, 0], gather.at[k, 2], gat_s.at[k, 2], gat_r.at[k, 2], (r, across))
        )
        near.append(
            send(gather.at[k, 0], gather.at[k, 1], gat_s.at[k, 1], gat_r.at[k, 1], (r, beside))
        )
    for k in range(req_size):
        over[k].wait_recv()
        far.append(
            send(gather.at[k, 2], gather.at[k, 3], gat_s.at[k, 3], gat_r.at[k, 3], (r, beside))
        )
    for k in range(req_size):
        near[k].wait_recv()
        far[k].wait_recv()
        values = [gather[k, i].astype(jnp.float32) for i in range(4)]
        mean = functools.reduce(
            jnp.add, [jnp.sum(v * v, axis=1, keepdims=True) for v in values]
        ) / (width * tp_size)
        scale = lax.rsqrt(mean + EPSILON)
        for i in range(4):
            cols = pl.ds(pl.multiple_of(owner[i] * width, 128), width)
            final_buf[k * rows : (k + 1) * rows, cols] = (
                values[i] * scale * final_gain_ref[:, cols]
            ).astype(jnp.bfloat16)
    load_head.wait()
    vocab = head_buf.shape[1]
    tile = min(512, vocab)
    each = rows // tp_size
    pairs = list(range(0, req_size, 2))
    pairs = sorted(pairs, key=lambda k: abs(k + 0.5 - req_size / 2))
    sent = []
    for first_k in pairs:

        def head_tile(c, carry, first_k=first_k):
            cols = pl.ds(pl.multiple_of(c * tile, 128), tile)
            part = jnp.dot(
                final_buf[first_k * rows : (first_k + 2) * rows, :], head_buf[:, cols],
                preferred_element_type=jnp.float32,
            ).astype(jnp.bfloat16)
            for i in range(2):
                for q in range(tp_size):
                    at = i * rows + q * each
                    logit_out[first_k + i, q, :, cols] = part[at : at + each, :]
            return carry

        lax.fori_loop(0, vocab // tile, head_tile, 0)
        for k in (first_k, first_k + 1):
            back = lax.rem(r + req_size - k, req_size)
            for q in range(tp_size):
                if k or q:
                    copy = send(
                        logit_out.at[k, peers[q]], logit_buf.at[k, q], log_s.at[k, q],
                        log_r.at[k, q], (back, peers[q]),
                    )
                    sent.append((k, q, copy))

    def place(value, k, q):
        source = reqs[k] * tp_size + lax.rem(t + tp_size - q, tp_size)
        cols = pl.ds(pl.multiple_of(source * vocab, 128), vocab)
        logits_ref[:, cols] = value.astype(jnp.float32)

    place(logit_out[0, t], 0, 0)
    for k, q, copy in sorted(sent, key=lambda item: min(item[0], req_size - item[0])):
        copy.wait_recv()
        place(logit_buf[k, q], k, q)
    for k, q, copy in sent:
        copy.wait_send()
    for k in range(req_size):
        if k:
            along[k].wait_send()
        over[k].wait_send()
        near[k].wait_send()
        far[k].wait_send()


def joint(
    summed, stats, gated, mixer_gain, mamba_out, attention_out, residual, final_gain, output_head
):
    tp_size = lax.axis_size("tp")
    req_size = lax.axis_size("req")
    rows, model = residual.shape
    width = model // tp_size
    chunk = summed.shape[2]
    each = rows // tp_size
    vocab = output_head.shape[1]
    dma = lambda *shape: pltpu.SemaphoreType.DMA(shape)
    vmem = pl.BlockSpec(memory_space=pltpu.VMEM)
    return pl.pallas_call(
        functools.partial(joint_kernel, tp_size, req_size),
        in_specs=[vmem] * 8 + [pl.BlockSpec(memory_space=pl.ANY)],
        out_specs=[vmem] * 2,
        out_shape=[
            jax.ShapeDtypeStruct((rows, width), jnp.bfloat16),
            jax.ShapeDtypeStruct((each, vocab * req_size * tp_size), jnp.float32),
        ],
        scratch_shapes=[
            pltpu.VMEM((tp_size, rows, chunk), jnp.bfloat16),
            pltpu.VMEM((tp_size, rows, 128), jnp.float32),
            pltpu.VMEM((tp_size, rows, width), jnp.bfloat16),
            pltpu.VMEM((tp_size, rows, width), jnp.bfloat16),
            pltpu.VMEM((req_size, 4, rows, width), jnp.bfloat16),
            pltpu.VMEM((req_size * rows, model), jnp.bfloat16),
            pltpu.VMEM(output_head.shape, jnp.bfloat16),
            pltpu.VMEM((req_size, tp_size, each, vocab), jnp.bfloat16),
            pltpu.VMEM((req_size, tp_size, each, vocab), jnp.bfloat16),
            dma(tp_size), dma(tp_size), dma(tp_size), dma(tp_size), dma(tp_size), dma(tp_size),
            dma(req_size, 4), dma(req_size, 4), dma(req_size, tp_size), dma(req_size, tp_size),
            dma(1),
        ],
        compiler_params=pltpu.CompilerParams(
            collective_id=1, has_side_effects=True, vmem_limit_bytes=40 << 20
        ),
    )(summed, stats, gated, mixer_gain[None], mamba_out, attention_out, residual, final_gain[None], output_head)


def body(
    residual,
    cache_lengths,
    input_gain,
    inner_weight,
    step_weight,
    step_bias,
    decay_log,
    skip_gain,
    conv_weight,
    conv_state,
    coupling_weight,
    coupling_conv,
    coupling_state,
    scan_state,
    mixer_gain,
    attention_weight,
    sink_cache,
    window_cache,
    mamba_out,
    attention_out,
    final_gain,
    output_head,
):
    row_count = residual.shape[0]
    tp_size = lax.axis_size("tp")
    local_units = inner_weight.shape[2]
    swap = lambda array: jnp.transpose(array, (1, 0, 2))
    coup_state = swap(coupling_state)
    normed, coupling_pre, qkv_rows, coupling_all, step_size, decay_rate = entry(
        step_bias, decay_log, residual, input_gain, attention_weight, coupling_weight,
        coupling_conv, coup_state, step_weight.T,
    )
    projected = jnp.einsum(
        "rd,dtc->trc", normed, inner_weight, preferred_element_type=jnp.float32
    ).astype(jnp.bfloat16)
    new_key_value = qkv_rows[:, QH * HD :]
    new_state, new_conv, new_coup, summed, stats, gated = mixer(
        cache_lengths, skip_gain, qkv_rows, sink_cache, window_cache,
        scan_state.reshape(row_count, local_units, NS), coupling_all, coupling_pre, coup_state,
        projected, conv_weight, swap(conv_state), step_size, decay_rate, tp_size,
    )
    new_conv_state = swap(new_conv)
    new_coupling_state = swap(new_coup)
    new_scan_state = new_state.reshape(scan_state.shape)
    new_residual, logits = joint(
        summed, stats, gated, mixer_gain, mamba_out, attention_out, residual, final_gain, output_head
    )
    return (new_residual, logits, new_scan_state, new_conv_state, new_coupling_state, new_key_value)


def solution(mesh):
    return jax.shard_map(
        body,
        mesh=mesh,
        in_specs=(
            P("req", None),
            P("req"),
            P(),
            P(None, None, "tp"),
            P(None, "tp"),
            P("tp"),
            P("tp"),
            P("tp"),
            P(None, "tp"),
            P("req", None, "tp"),
            P(None, "tp"),
            P(None, "tp"),
            P("req", None, "tp"),
            P("req", "tp", None, None),
            P("tp"),
            P(None, "tp"),
            P("req", None, None),
            P("req", "tp", None),
            P("tp", None),
            P("tp", None),
            P(),
            P(None, ("req", "tp")),
        ),
        out_specs=(
            P("req", "tp"),
            P(("req", "tp"), None),
            P("req", "tp", None, None),
            P("req", None, "tp"),
            P("req", None, "tp"),
            P("req", None),
        ),
        check_vma=False,
    )
```

```python
import functools

import jax
import jax.numpy as jnp
from jax import lax
from jax.experimental import pallas as pl
from jax.experimental.pallas import tpu as pltpu
from jax.sharding import PartitionSpec as P

MH = 24
MP = 64
NS = 256
QH = 8
KVH = 2
HD = 128
WIN = 1024
SINK = 4
BR = 8
EXTRA = 16

EPSILON = 1e-05
NEG_BIG = -1e30
MESH = pl.DeviceIdType.MESH
NT = (((1,), (1,)), ((), ()))


def norm_rows(values, gain):
    widened = values.astype(jnp.float32)
    mean_sq = jnp.mean(widened * widened, axis=-1, keepdims=True)
    return (widened * lax.rsqrt(mean_sq + EPSILON) * gain).astype(jnp.bfloat16)


def silu(v):
    return v / (1.0 + jnp.exp(-v))


def conv_rows(state_ref, fresh, taps_ref):
    steps = [state_ref[k].astype(jnp.float32) for k in range(3)] + [fresh.astype(jnp.float32)]
    taps = taps_ref[...].astype(jnp.float32)
    mixed = steps[0] * taps[0:1]
    for k in range(1, 4):
        mixed = mixed + steps[k] * taps[k : k + 1]
    return silu(mixed)


def by_head(ref, g, shape):
    lane = lax.broadcasted_iota(jnp.int32, shape, 1)
    return jnp.where(lane < MP, ref[2 * g], ref[2 * g + 1])


def entry_kernel(
    tp_size, bias_ref, log_ref, residual_ref, gain_ref, attention_ref, coupling_ref, taps_ref,
    state_ref, step_weight_ref, normed_ref, pre_ref, qkv_ref, coup_ref, step_ref, decay_ref,
    qkv_s, qkv_r, coup_s, coup_r,
):
    r = lax.axis_index("req")
    t = lax.axis_index("tp")
    peers = [lax.rem(t + k, tp_size) for k in range(tp_size)]
    barrier = pltpu.get_barrier_semaphore()
    for k in range(1, tp_size):
        pl.semaphore_signal(barrier, inc=1, device_id=(r, peers[k]), device_id_type=MESH)
    normed = norm_rows(residual_ref[...], gain_ref[...])
    normed_ref[...] = normed
    copies = []

    def share(out_ref, value, ssem, rsem):
        width = value.shape[1]
        cols = pl.ds(pl.multiple_of(t * width, 128), width)
        out_ref[:, cols] = value
        for k in range(1, tp_size):
            copy = pltpu.make_async_remote_copy(
                src_ref=out_ref.at[:, cols], dst_ref=out_ref.at[:, cols], send_sem=ssem.at[k],
                recv_sem=rsem.at[k], device_id=(r, peers[k]), device_id_type=MESH,
            )
            copy.start()
            copies.append(copy)

    qkv = jnp.dot(normed, attention_ref[...], preferred_element_type=jnp.float32)
    pl.semaphore_wait(barrier, tp_size - 1)
    share(qkv_ref, qkv.astype(jnp.bfloat16), qkv_s, qkv_r)
    pre = jnp.dot(normed, coupling_ref[...], preferred_element_type=jnp.float32).astype(jnp.bfloat16)
    pre_ref[...] = pre
    share(coup_ref, conv_rows(state_ref, pre, taps_ref).astype(jnp.bfloat16), coup_s, coup_r)
    steps = (
        lax.dot_general(normed, step_weight_ref[...], NT, preferred_element_type=jnp.float32)
        .astype(jnp.bfloat16)
        .astype(jnp.float32)
    )
    shape = (normed.shape[0], 2 * MP)
    for g in range(steps.shape[1] // 2):
        lane = lax.broadcasted_iota(jnp.int32, shape, 1)
        v = jnp.where(lane < MP, steps[:, 2 * g : 2 * g + 1], steps[:, 2 * g + 1 : 2 * g + 2])
        v = v + by_head(bias_ref, g, shape)
        size = jnp.maximum(v, 0.0) + jnp.log1p(jnp.exp(-jnp.abs(v)))
        step_ref[:, g * 2 * MP : (g + 1) * 2 * MP] = size
        decay_ref[:, g * 2 * MP : (g + 1) * 2 * MP] = jnp.exp(
            -size * jnp.exp(by_head(log_ref, g, shape))
        )
    for copy in copies:
        copy.wait()


def entry(bias, decay_log, residual, gain, attention_weight, coupling_weight, taps, state, step_weight):
    tp_size = lax.axis_size("tp")
    rows, model = residual.shape
    units = bias.shape[0] * MP
    vmem = pl.BlockSpec(memory_space=pltpu.VMEM)
    smem = pl.BlockSpec(memory_space=pltpu.SMEM)
    dma = pltpu.SemaphoreType.DMA((tp_size,))
    shaped = jax.ShapeDtypeStruct
    return pl.pallas_call(
        functools.partial(entry_kernel, tp_size),
        in_specs=[smem] * 2 + [vmem] * 7,
        out_specs=[vmem] * 6,
        out_shape=[
            shaped((rows, model), jnp.bfloat16),
            shaped((rows, coupling_weight.shape[1]), jnp.bfloat16),
            shaped((rows, attention_weight.shape[1] * tp_size), jnp.bfloat16),
            shaped((rows, coupling_weight.shape[1] * tp_size), jnp.bfloat16),
            shaped((rows, units), jnp.float32),
            shaped((rows, units), jnp.float32),
        ],
        scratch_shapes=[dma] * 4,
        compiler_params=pltpu.CompilerParams(
            collective_id=0, has_side_effects=True, vmem_limit_bytes=60 << 20
        ),
    )(bias, decay_log, residual, gain[None], attention_weight, coupling_weight, taps, state, step_weight)


def mixer_kernel(
    len_ref, skip_ref, qkv_ref, sink_ref, window_ref, state_ref, coup_ref, pre_ref, coup_state_ref,
    projected_ref, taps_ref, conv_state_ref, step_ref, decay_ref, new_state_ref, new_conv_ref,
    new_coup_ref, summed_ref, stats_ref, gated_ref, heads_scr, extra_scr,
):
    half = KVH * HD
    group = QH // KVH
    t = lax.axis_index("tp")
    for h in range(QH):
        heads_scr[pl.ds(h, BR, stride=QH), :] = qkv_ref[:, h * HD : (h + 1) * HD].astype(jnp.float32)
    extra_scr[...] = jnp.zeros_like(extra_scr)
    fresh_rows = qkv_ref[:, QH * HD :].astype(jnp.float32)
    units = step_ref.shape[1]
    gate = projected_ref[0].astype(jnp.float32)
    x_pre = projected_ref[1]
    x = conv_rows(conv_state_ref, x_pre, taps_ref)
    new_conv_ref[0] = conv_state_ref[1]
    new_conv_ref[1] = conv_state_ref[2]
    new_conv_ref[2] = x_pre
    new_coup_ref[0] = coup_state_ref[1]
    new_coup_ref[1] = coup_state_ref[2]
    new_coup_ref[2] = pre_ref[...]
    head_row = lax.broadcasted_iota(jnp.int32, (QH, HD), 0)
    lane = lax.broadcasted_iota(jnp.int32, (QH, HD), 1)
    first_half = head_row < group
    step_x = step_ref[...] * x
    decay = decay_ref[...]
    step_x_t = step_x.T
    decay_t = decay.T
    coup = coup_ref[...]
    out_rows = coup[:, NS:]
    in_f32 = coup[:, :NS].astype(jnp.float32)
    both = jnp.sum(in_f32 * out_rows.astype(jnp.float32), axis=1, keepdims=True)
    read_rows = []
    for j in range(BR):
        q = heads_scr[j * QH : (j + 1) * QH, :]
        wide = jnp.concatenate(
            [jnp.where(first_half, q, 0.0), jnp.where(first_half, 0.0, q)], axis=1
        ).astype(jnp.bfloat16)
        extra_scr[j, :SINK, :] = sink_ref[j].astype(jnp.float32)
        extra_scr[j, SINK : SINK + 1, :] = fresh_rows[j : j + 1, :]
        extra = extra_scr[j].astype(jnp.bfloat16)
        s1 = lax.dot_general(
            wide, window_ref[j, :, :half], NT, preferred_element_type=jnp.float32
        ) * HD ** (-0.5)
        s2 = lax.dot_general(
            wide, extra[:, :half], NT, preferred_element_type=jnp.float32
        ) * HD ** (-0.5)
        last = len_ref[pl.program_id(0) * BR + j] - 1
        slots = window_ref.shape[1]
        slot = t * slots + lax.broadcasted_iota(jnp.int32, s1.shape, 1)
        back = jnp.bitwise_and(last - slot, WIN - 1)
        live1 = (last - back >= SINK) & (back != WIN - 1)
        live2 = lax.broadcasted_iota(jnp.int32, s2.shape, 1) < jnp.where(t == 0, SINK + 1, 0)
        s1 = jnp.where(live1, s1, NEG_BIG)
        s2 = jnp.where(live2, s2, NEG_BIG)
        peak = jnp.maximum(
            jnp.max(s1, axis=1, keepdims=True), jnp.max(s2, axis=1, keepdims=True)
        )
        w1 = jnp.where(live1, jnp.exp(s1 - peak), 0.0)
        w2 = jnp.where(live2, jnp.exp(s2 - peak), 0.0)
        total = jnp.sum(w1, axis=1, keepdims=True) + jnp.sum(w2, axis=1, keepdims=True)
        acc = jnp.dot(
            w1.astype(jnp.bfloat16), window_ref[j, :, half:], preferred_element_type=jnp.float32
        ) + jnp.dot(
            w2.astype(jnp.bfloat16), extra[:, half:], preferred_element_type=jnp.float32
        )
        heads_scr[j * QH : (j + 1) * QH, :] = jnp.where(first_half, acc[:, :HD], acc[:, HD:])
        stats_ref[j : j + 1, :] = jnp.sum(
            jnp.where(lane == head_row, peak, 0.0)
            + jnp.where(lane == head_row + QH, total, 0.0),
            axis=0,
            keepdims=True,
        )
        state = state_ref[j]
        read_rows.append(
            lax.dot_general(out_rows, state, NT, preferred_element_type=jnp.float32)[j : j + 1, :]
        )
        new_state_ref[j] = (
            decay_t[:, j : j + 1] * state.astype(jnp.float32)
            + step_x_t[:, j : j + 1] * in_f32[j : j + 1, :]
        ).astype(jnp.bfloat16)
    per_chunk = summed_ref.shape[2] // HD
    for h in range(QH):
        summed_ref[h // per_chunk, :, (h % per_chunk) * HD : (h % per_chunk + 1) * HD] = heads_scr[
            pl.ds(h, BR, stride=QH), :
        ].astype(jnp.bfloat16)
    readout = decay * jnp.concatenate(read_rows, axis=0) + step_x * both
    skip = jnp.concatenate(
        [by_head(skip_ref, g, (BR, 2 * MP)) for g in range(units // (2 * MP))], axis=1
    )
    gated = (readout + skip * x) * silu(gate)
    gated_ref[...] = gated
    square = jnp.sum(gated * gated, axis=1, keepdims=True)
    stats_ref[...] = jnp.where(
        lax.broadcasted_iota(jnp.int32, stats_ref.shape, 1) == 2 * QH, square, stats_ref[...]
    )


def mixer(
    lengths, skip, qkv, sink, window, state, coup, pre, coup_state, projected, taps, conv_state,
    step, decay, tp_size,
):
    rows, units = step.shape
    row = lambda a: pl.BlockSpec((BR, a.shape[1]), lambda i: (i, 0))
    cube = lambda a: pl.BlockSpec((BR,) + a.shape[1:], lambda i: (i, 0, 0))
    steps = lambda a: pl.BlockSpec((3, BR, a.shape[2]), lambda i: (0, i, 0))
    smem = pl.BlockSpec(memory_space=pltpu.SMEM)
    chunk = QH * HD // tp_size
    return pl.pallas_call(
        mixer_kernel,
        grid=(rows // BR,),
        in_specs=[
            smem, smem, row(qkv), cube(sink), cube(window), cube(state), row(coup), row(pre),
            steps(coup_state), pl.BlockSpec((2, BR, units), lambda i: (0, i, 0)), pl.BlockSpec(taps.shape, lambda i: (0, 0)),
            steps(conv_state), row(step), row(decay),
        ],
        out_specs=[
            cube(state), steps(conv_state), steps(coup_state),
            pl.BlockSpec((tp_size, BR, chunk), lambda i: (0, i, 0)),
            pl.BlockSpec((BR, 128), lambda i: (i, 0)), row(step),
        ],
        out_shape=[
            jax.ShapeDtypeStruct(state.shape, jnp.bfloat16),
            jax.ShapeDtypeStruct(conv_state.shape, jnp.bfloat16),
            jax.ShapeDtypeStruct(coup_state.shape, jnp.bfloat16),
            jax.ShapeDtypeStruct((tp_size, rows, chunk), jnp.bfloat16),
            jax.ShapeDtypeStruct((rows, 128), jnp.float32),
            jax.ShapeDtypeStruct((rows, units), jnp.float32),
        ],
        scratch_shapes=[
            pltpu.VMEM((BR * QH, HD), jnp.float32),
            pltpu.VMEM((BR, EXTRA, 2 * KVH * HD), jnp.float32),
        ],
        compiler_params=pltpu.CompilerParams(vmem_limit_bytes=60 << 20),
    )(
        lengths, skip, qkv, sink, window, state, coup, pre, coup_state, projected, taps, conv_state,
        step, decay,
    )


def joint_kernel(
    tp_size, req_size, summed_ref, stats_ref, gated_ref, mixer_gain_ref, mamba_out_ref,
    attention_out_ref, residual_ref, final_gain_ref, head_ref, new_residual_ref, logits_ref,
    sum_buf, stat_buf, part_out, part_buf, gather, final_buf, head_buf, logit_out, logit_buf,
    sum_s, sum_r, stat_s, stat_r, part_s, part_r, gat_s, gat_r, log_s, log_r, head_sem,
):
    r = lax.axis_index("req")
    t = lax.axis_index("tp")
    rows = gated_ref.shape[0]
    width = new_residual_ref.shape[1]
    peers = [lax.rem(t + k, tp_size) for k in range(tp_size)]
    reqs = [lax.rem(r + k, req_size) for k in range(req_size)]
    barrier = pltpu.get_barrier_semaphore()
    load_head = pltpu.make_async_copy(head_ref, head_buf, head_sem.at[0])
    load_head.start()
    for k in range(req_size):
        for q in range(tp_size):
            if k or q:
                pl.semaphore_signal(
                    barrier, inc=1, device_id=(reqs[k], peers[q]), device_id_type=MESH
                )
    pl.semaphore_wait(barrier, tp_size * req_size - 1)

    def send(src, dst, ssem, rsem, where):
        copy = pltpu.make_async_remote_copy(
            src_ref=src, dst_ref=dst, send_sem=ssem, recv_sem=rsem,
            device_id=where, device_id_type=MESH,
        )
        copy.start()
        return copy

    first = []
    for k in range(1, tp_size):
        where = (r, peers[k])
        first.append(send(stats_ref, stat_buf.at[k], stat_s.at[k], stat_r.at[k], where))
        first.append(send(summed_ref.at[peers[k]], sum_buf.at[k], sum_s.at[k], sum_r.at[k], where))
    for copy in first:
        copy.wait()
    stats = [stats_ref[...]] + [stat_buf[k] for k in range(1, tp_size)]
    sums = [summed_ref[t].astype(jnp.float32)] + [
        sum_buf[k].astype(jnp.float32) for k in range(1, tp_size)
    ]
    lane = lax.broadcasted_iota(jnp.int32, (rows, 128), 1)
    local_heads = QH // tp_size
    pieces = []
    for hl in range(local_heads):
        h = t * local_heads + hl
        peaks = [jnp.sum(jnp.where(lane == h, s, 0.0), axis=1, keepdims=True) for s in stats]
        totals = [jnp.sum(jnp.where(lane == h + QH, s, 0.0), axis=1, keepdims=True) for s in stats]
        top = functools.reduce(jnp.maximum, peaks)
        scales = [jnp.exp(p - top) for p in peaks]
        below = functools.reduce(jnp.add, [a * b for a, b in zip(scales, totals)])
        above = functools.reduce(
            jnp.add, [a * b[:, hl * HD : (hl + 1) * HD] for a, b in zip(scales, sums)]
        )
        pieces.append((above / below).astype(jnp.bfloat16))
    attended = jnp.concatenate(pieces, axis=1)
    square = functools.reduce(jnp.add, [s[:, 2 * QH : 2 * QH + 1] for s in stats])
    mamba = (
        gated_ref[...] * lax.rsqrt(square / (MH * MP) + EPSILON) * mixer_gain_ref[...]
    ).astype(jnp.bfloat16)

    def partial(p):
        cols = pl.ds(pl.multiple_of(p * width, 128), width)
        return jnp.dot(mamba, mamba_out_ref[:, cols], preferred_element_type=jnp.float32) + jnp.dot(
            attended, attention_out_ref[:, cols], preferred_element_type=jnp.float32
        )

    second = []
    for k in range(1, tp_size):
        part_out[k] = partial(peers[k]).astype(jnp.bfloat16)
        second.append(
            send(part_out.at[k], part_buf.at[k], part_s.at[k], part_r.at[k], (r, peers[k]))
        )
    mixed = partial(t)
    for k in range(1, tp_size):
        second[k - 1].wait()
        mixed = mixed + part_buf[k].astype(jnp.float32)
    own = pl.ds(pl.multiple_of(t * width, 128), width)
    fresh = (residual_ref[:, own].astype(jnp.float32) + mixed).astype(jnp.bfloat16)
    new_residual_ref[...] = fresh
    gather[0, 0] = fresh

    beside = t + 1 - 2 * lax.rem(t, 2)
    across = lax.rem(t + 2, tp_size)
    owner = [t, beside, across, lax.rem(beside + 2, tp_size)]
    along = [None]
    for k in range(1, req_size):
        along.append(
            send(gather.at[0, 0], gather.at[k, 0], gat_s.at[k, 0], gat_r.at[k, 0], (reqs[k], t))
        )
    over, near, far = [], [], []
    for k in range(req_size):
        if k:
            along[k].wait_recv()
        over.append(
            send(gather.at[k, 0], gather.at[k, 2], gat_s.at[k, 2], gat_r.at[k, 2], (r, across))
        )
        near.append(
            send(gather.at[k, 0], gather.at[k, 1], gat_s.at[k, 1], gat_r.at[k, 1], (r, beside))
        )
    for k in range(req_size):
        over[k].wait_recv()
        far.append(
            send(gather.at[k, 2], gather.at[k, 3], gat_s.at[k, 3], gat_r.at[k, 3], (r, beside))
        )
    for k in range(req_size):
        near[k].wait_recv()
        far[k].wait_recv()
        values = [gather[k, i].astype(jnp.float32) for i in range(4)]
        mean = functools.reduce(
            jnp.add, [jnp.sum(v * v, axis=1, keepdims=True) for v in values]
        ) / (width * tp_size)
        scale = lax.rsqrt(mean + EPSILON)
        for i in range(4):
            cols = pl.ds(pl.multiple_of(owner[i] * width, 128), width)
            final_buf[k * rows : (k + 1) * rows, cols] = (
                values[i] * scale * final_gain_ref[:, cols]
            ).astype(jnp.bfloat16)
    load_head.wait()
    vocab = head_buf.shape[1]
    tile = min(512, vocab)
    each = rows // tp_size
    pairs = list(range(0, req_size, 2))
    pairs = sorted(pairs, key=lambda k: abs(k + 0.5 - req_size / 2))
    sent = []
    for first_k in pairs:

        def head_tile(c, carry, first_k=first_k):
            cols = pl.ds(pl.multiple_of(c * tile, 128), tile)
            part = jnp.dot(
                final_buf[first_k * rows : (first_k + 2) * rows, :], head_buf[:, cols],
                preferred_element_type=jnp.float32,
            ).astype(jnp.bfloat16)
            for i in range(2):
                for q in range(tp_size):
                    at = i * rows + q * each
                    logit_out[first_k + i, q, :, cols] = part[at : at + each, :]
            return carry

        lax.fori_loop(0, vocab // tile, head_tile, 0)
        for k in (first_k, first_k + 1):
            back = lax.rem(r + req_size - k, req_size)
            for q in range(tp_size):
                if k or q:
                    copy = send(
                        logit_out.at[k, peers[q]], logit_buf.at[k, q], log_s.at[k, q],
                        log_r.at[k, q], (back, peers[q]),
                    )
                    sent.append((k, q, copy))

    def place(value, k, q):
        source = reqs[k] * tp_size + lax.rem(t + tp_size - q, tp_size)
        cols = pl.ds(pl.multiple_of(source * vocab, 128), vocab)
        logits_ref[:, cols] = value.astype(jnp.float32)

    place(logit_out[0, t], 0, 0)
    for k, q, copy in sorted(sent, key=lambda item: min(item[0], req_size - item[0])):
        copy.wait_recv()
        place(logit_buf[k, q], k, q)
    for k, q, copy in sent:
        copy.wait_send()
    for k in range(req_size):
        if k:
            along[k].wait_send()
        over[k].wait_send()
        near[k].wait_send()
        far[k].wait_send()


def joint(
    summed, stats, gated, mixer_gain, mamba_out, attention_out, residual, final_gain, output_head
):
    tp_size = lax.axis_size("tp")
    req_size = lax.axis_size("req")
    rows, model = residual.shape
    width = model // tp_size
    chunk = summed.shape[2]
    each = rows // tp_size
    vocab = output_head.shape[1]
    dma = lambda *shape: pltpu.SemaphoreType.DMA(shape)
    vmem = pl.BlockSpec(memory_space=pltpu.VMEM)
    return pl.pallas_call(
        functools.partial(joint_kernel, tp_size, req_size),
        in_specs=[vmem] * 8 + [pl.BlockSpec(memory_space=pl.ANY)],
        out_specs=[vmem] * 2,
        out_shape=[
            jax.ShapeDtypeStruct((rows, width), jnp.bfloat16),
            jax.ShapeDtypeStruct((each, vocab * req_size * tp_size), jnp.float32),
        ],
        scratch_shapes=[
            pltpu.VMEM((tp_size, rows, chunk), jnp.bfloat16),
            pltpu.VMEM((tp_size, rows, 128), jnp.float32),
            pltpu.VMEM((tp_size, rows, width), jnp.bfloat16),
            pltpu.VMEM((tp_size, rows, width), jnp.bfloat16),
            pltpu.VMEM((req_size, 4, rows, width), jnp.bfloat16),
            pltpu.VMEM((req_size * rows, model), jnp.bfloat16),
            pltpu.VMEM(output_head.shape, jnp.bfloat16),
            pltpu.VMEM((req_size, tp_size, each, vocab), jnp.bfloat16),
            pltpu.VMEM((req_size, tp_size, each, vocab), jnp.bfloat16),
            dma(tp_size), dma(tp_size), dma(tp_size), dma(tp_size), dma(tp_size), dma(tp_size),
            dma(req_size, 4), dma(req_size, 4), dma(req_size, tp_size), dma(req_size, tp_size),
            dma(1),
        ],
        compiler_params=pltpu.CompilerParams(
            collective_id=1, has_side_effects=True, vmem_limit_bytes=60 << 20
        ),
    )(summed, stats, gated, mixer_gain[None], mamba_out, attention_out, residual, final_gain[None], output_head)


def body(
    residual,
    cache_lengths,
    input_gain,
    inner_weight,
    step_weight,
    step_bias,
    decay_log,
    skip_gain,
    conv_weight,
    conv_state,
    coupling_weight,
    coupling_conv,
    coupling_state,
    scan_state,
    mixer_gain,
    attention_weight,
    sink_cache,
    window_cache,
    mamba_out,
    attention_out,
    final_gain,
    output_head,
):
    row_count = residual.shape[0]
    tp_size = lax.axis_size("tp")
    local_units = inner_weight.shape[2]
    swap = lambda array: jnp.transpose(array, (1, 0, 2))
    coup_state = swap(coupling_state)
    normed, coupling_pre, qkv_rows, coupling_all, step_size, decay_rate = entry(
        step_bias, decay_log, residual, input_gain, attention_weight, coupling_weight,
        coupling_conv, coup_state, step_weight.T,
    )
    projected = jnp.einsum(
        "rd,dtc->trc", normed, inner_weight, preferred_element_type=jnp.float32
    ).astype(jnp.bfloat16)
    new_key_value = qkv_rows[:, QH * HD :]
    new_state, new_conv, new_coup, summed, stats, gated = mixer(
        cache_lengths, skip_gain, qkv_rows, sink_cache, window_cache,
        scan_state.reshape(row_count, local_units, NS), coupling_all, coupling_pre, coup_state,
        projected, conv_weight, swap(conv_state), step_size, decay_rate, tp_size,
    )
    new_conv_state = swap(new_conv)
    new_coupling_state = swap(new_coup)
    new_scan_state = new_state.reshape(scan_state.shape)
    new_residual, logits = joint(
        summed, stats, gated, mixer_gain, mamba_out, attention_out, residual, final_gain, output_head
    )
    return (new_residual, logits, new_scan_state, new_conv_state, new_coupling_state, new_key_value)


def solution(mesh):
    return jax.shard_map(
        body,
        mesh=mesh,
        in_specs=(
            P("req", None),
            P("req"),
            P(),
            P(None, None, "tp"),
            P(None, "tp"),
            P("tp"),
            P("tp"),
            P("tp"),
            P(None, "tp"),
            P("req", None, "tp"),
            P(None, "tp"),
            P(None, "tp"),
            P("req", None, "tp"),
            P("req", "tp", None, None),
            P("tp"),
            P(None, "tp"),
            P("req", None, None),
            P("req", "tp", None),
            P("tp", None),
            P("tp", None),
            P(),
            P(None, ("req", "tp")),
        ),
        out_specs=(
            P("req", "tp"),
            P(("req", "tp"), None),
            P("req", "tp", None, None),
            P("req", None, "tp"),
            P("req", None, "tp"),
            P("req", None),
        ),
        check_vma=False,
    )
```
